32 devices in a mesh: groups: 2 (over x), expert: 16 (over z, y, core).
Axes of the slice: x: 2, y: 2, z: 4, core: 2. Of those that a mesh axis runs over, the one named last changes fastest.
Arguments:
- hidden_states: bfloat16 [2, 512, 4096], P(None, ('groups', 'expert')), parts along dimension 1, may hold values from -6 to 6
- expert_ids: int32 [2, 512, 8], P(None, ('groups', 'expert')), parts along dimension 1, may hold values from 0 to 15, all different within a row; in each aligned block of 16 rows (0 to 15, 16 to 31, ..., all dimensions but the last counted through in order) at most 16 rows name the same one
- router_probs: float32 [2, 512, 8], P(None, ('groups', 'expert')), parts along dimension 1, may hold values from 0.05 to 1
- swap_flags: int32 [16], replicated, may hold values from 0 to 1, as said below
- w_gate: bfloat16 [16, 4096, 768], P('expert'), may hold values from -0.09375 to 0.09375
- w_up: bfloat16 [16, 4096, 768], P('expert'), may hold values from -0.09375 to 0.09375
- w_down: bfloat16 [16, 768, 4096], P('expert'), may hold values from -0.21875 to 0.21875
Outputs:
- mixed: bfloat16 [2, 512, 4096], P(None, ('groups', 'expert')), parts along dimension 1
The draws below stay inside these ranges and needn't reach their ends.
There are 2 independent parts, one for each index of `groups`. The reference program is written for one: setup_inputs(seed, part) draws one part's arguments, and reference() takes and returns one part's arrays. A program takes and returns all parts, laid end to end along the dimension named above; an argument that names none is the same for every part. Nothing has to cross between parts.
Inputs may be any that keep to these rules, and one draw needn't show every extreme that they name: `expert_ids`: within one step, the 16 rows of one device (aligned blocks of 16 rows) name any one slot at most 16 times, a bound that some block reaches; the 8 ids of a row differ. swap_flags[e] equals swap_flags[e XOR 1] for every slot e.
All inputs are finite; a program needn't handle non-finite values.
Results may differ from the reference program's by a relative error of at most 0.0058.
Values may be sent and summed in bfloat16 or wider, within the bound.
A program may use at most 128 MiB of HBM per device.

```python
import math
import jax
import jax.numpy as jnp
import numpy as np
from jax import lax

D = 4096
FW = 768
TOPK = 8
STEPS = 2
TOK_DEV = 16
EXPERTS = 16
TOKENS = 256
CAP = 16
N_EXPERT = 16


def draw_swap_flags(key, part):
    pair_flags = jax.random.randint(jax.random.fold_in(key, 7), (EXPERTS // 2,), 0, 2).astype(jnp.int32)
    return jnp.repeat(pair_flags, 2).astype(jnp.int32)


def block_scale(own_key, shape, shards, low, high):
    level, own = 1.0, jax.random.fold_in(own_key, 6)
    for dim, parts in shards:
        steps = jnp.exp(jax.random.uniform(jax.random.fold_in(own, dim), (parts,), jnp.float32, low / len(shards), high / len(shards)))
        level = level * jnp.repeat(steps, shape[dim] // parts).reshape([-1 if axis == dim else 1 for axis in range(len(shape))])
    return level


def routed_block(own_key, own, number, rows, number_of, top, bound, skew):
    sequence = jax.random.permutation(own_key, number_of)
    crowded, usual = load_shares(number_of, rows * top, bound, skew, True), load_shares(number_of, rows * top, bound, skew, False)
    places = jnp.arange(number_of)

    def named(tallies, offset_by):
        used = int((tallies > 0).sum())
        fixed = max(1, used // 4)
        shifted = fixed + (places - fixed + offset_by * (used - fixed)) % max(1, number_of - fixed)
        return jnp.zeros((number_of,), jnp.int32).at[sequence[jnp.where(places < fixed, places, shifted)]].set(jnp.asarray(tallies, jnp.int32))

    tallies = jnp.where(number % 4 == 0, named(crowded, number // 4), named(usual, number - number // 4 - 1))
    mixed = jax.random.permutation(jax.random.fold_in(own, 3), number_of)
    source_of, taker = mixed[0:number_of // 2 * 2:2], mixed[1:number_of // 2 * 2:2]
    margin = jnp.minimum(tallies[source_of] - 1, bound - tallies[taker]) // 2
    margin = jnp.where((source_of == sequence[0]) | (taker == sequence[0]) | (tallies[taker] == 0), 0, jnp.maximum(margin, 0))
    shifted = jax.random.randint(jax.random.fold_in(own, 4), (number_of // 2,), 0, 1 << 20) % (margin + 1)
    tallies = tallies.at[source_of].add(-shifted).at[taker].add(shifted)
    members = jnp.searchsorted(jnp.cumsum(tallies), jnp.arange(rows * top), side="right").astype(jnp.int32)
    listing = members.reshape(top, rows).T
    listing = listing[jax.random.permutation(jax.random.fold_in(own, 1), rows)]
    offset_by = jax.random.randint(jax.random.fold_in(own, 2), (rows, 1), 0, top)
    return jnp.take_along_axis(listing, (jnp.arange(top)[None, :] + offset_by) % top, axis=1)


def load_shares(number_of, total, bound, slope, full):
    portions = [(1 << 20) // math.isqrt(grade ** slope) + 1 for grade in range(1, number_of + 1)]
    largest = bound if full else min(bound, max(-(-total // number_of), total * portions[0] // sum(portions)))
    least = 1 if total - largest >= number_of - 1 else 0
    holding, spare = [largest] + [least] * (number_of - 1), total - largest - least * (number_of - 1)
    while spare > 0:
        movable = [i for i in range(1, number_of) if holding[i] < largest] or [i for i in range(1, number_of) if holding[i] < bound]
        whole, budget = sum([portions[i] for i in movable]), spare
        for i in movable:
            more = min(bound - holding[i], max(1, budget * portions[i] // whole), spare)
            holding[i] = holding[i] + more
            spare = spare - more
    return np.array(holding)


def scatter_about(rng, extent, scale, bound, pieces=(), kind=jnp.bfloat16):
    entries = scale * jax.random.normal(rng, extent, jnp.float32)
    if pieces:
        entries = entries * block_scale(rng, extent, pieces, -0.22, 0.18)
    return jnp.clip(entries, -bound, bound).astype(kind)


def setup_inputs(seed: int = 0, part: int = 0) -> dict:
    key_list = jax.random.split(jax.random.key(seed), 8)
    part_keys = jax.random.split(jax.random.fold_in(key_list[7], part), 8)
    hidden_states = scatter_about(part_keys[0], (STEPS, TOKENS, D), 1.0, 6.0, ((1, 16),))
    expert_ids_keys = jax.random.split(jax.random.fold_in(part_keys[1], 1), STEPS * TOKENS // TOK_DEV)
    expert_ids_turns = jax.random.permutation(jax.random.fold_in(part_keys[1], 3), STEPS * TOKENS // TOK_DEV)
    expert_ids = jax.vmap(lambda own, number: routed_block(jax.random.fold_in(part_keys[1], 2), own, number, TOK_DEV, EXPERTS, TOPK, CAP, 2))(expert_ids_keys, expert_ids_turns).reshape((STEPS, TOKENS, TOPK))
    router_probs = jnp.clip(jnp.exp(math.log(1.0) - 2.9957323 * jax.random.uniform(part_keys[2], (STEPS, TOKENS, TOPK), jnp.float32) ** block_scale(part_keys[2], (STEPS, TOKENS, TOPK), ((1, 16),), -0.2, 0.2)), 0.05, 1.0)
    swap_flags = draw_swap_flags(jax.random.fold_in(key_list[7], 71), part)
    w_gate = scatter_about(key_list[4], (EXPERTS, D, FW), D ** -0.5, 0.09375, ((0, 16),))
    w_up = scatter_about(key_list[5], (EXPERTS, D, FW), D ** -0.5, 0.09375, ((0, 16),))
    w_down = scatter_about(key_list[6], (EXPERTS, FW, D), FW ** -0.5, 0.21875, ((0, 16),))
    return {"hidden_states": hidden_states, "expert_ids": expert_ids, "router_probs": router_probs, "swap_flags": swap_flags, "w_gate": w_gate, "w_up": w_up, "w_down": w_down}


def expert_mlp(rows, gate_matrix, up_matrix, down_matrix):
    gate = jnp.dot(rows, gate_matrix, preferred_element_type=jnp.float32)
    up_part = jnp.dot(rows, up_matrix, preferred_element_type=jnp.float32)
    hidden = (jax.nn.silu(gate) * up_part).astype(jnp.bfloat16)
    return jnp.dot(hidden, down_matrix, preferred_element_type=jnp.float32).astype(jnp.bfloat16)


def apply_expert(operands):
    return expert_mlp(operands[0], operands[1], operands[2], operands[3])


def reference(hidden_states, expert_ids, router_probs, swap_flags, w_gate, w_up, w_down):
    outputs = []
    slots_iota = jnp.arange(EXPERTS, dtype=jnp.int32)
    partner = jnp.bitwise_xor(slots_iota, 1).astype(jnp.int32)
    for step_index in range(STEPS):
        if step_index == 0:
            held = slots_iota
        else:
            held = jnp.where(swap_flags == 1, partner, slots_iota).astype(jnp.int32)
        states = hidden_states[step_index]
        routed = expert_ids[step_index]
        weights_raw = router_probs[step_index]
        shares = weights_raw / jnp.sum(weights_raw, axis=-1, keepdims=True)
        blocks = routed.reshape(N_EXPERT, TOK_DEV * TOPK)
        onehot = (blocks[:, :, None] == slots_iota[None, None, :]).astype(jnp.int32)
        before = (jnp.cumsum(onehot, axis=1).astype(jnp.int32) - onehot) * onehot
        slot_rank = jnp.sum(before, axis=2).astype(jnp.int32)
        source = jnp.arange(N_EXPERT, dtype=jnp.int32)[:, None]
        target = (blocks * (N_EXPERT * CAP) + source * CAP + slot_rank).reshape(-1).astype(jnp.int32)
        token_row = (source * TOK_DEV + jnp.arange(TOK_DEV * TOPK, dtype=jnp.int32)[None, :] // TOPK).reshape(-1).astype(jnp.int32)
        row_table = jnp.full((EXPERTS * N_EXPERT * CAP,), TOKENS, jnp.int32).at[target].set(token_row)
        padded = jnp.concatenate([states, jnp.zeros((1, D), jnp.bfloat16)], axis=0)
        gathered = padded[row_table].reshape(EXPERTS, N_EXPERT * CAP, D)
        results = lax.map(apply_expert, (gathered, w_gate[held], w_up[held], w_down[held]))
        picked = results.reshape(-1, D)[target].reshape(TOKENS, TOPK, D).astype(jnp.float32)
        outputs.append(jnp.sum(shares[:, :, None] * picked, axis=1).astype(jnp.bfloat16))
    return jnp.stack(outputs)
```

```python
import functools

import jax
import jax.numpy as jnp
from jax import lax
from jax.experimental import pallas as pl
from jax.experimental.pallas import tpu as pltpu
from jax.sharding import PartitionSpec as P

MESH = pl.DeviceIdType.MESH
F32 = jnp.float32
BF16 = jnp.bfloat16
LANES = 128


def column_units(width):
    q, e = width // 4, width // 8
    return [(0, q, False), (q, q, False), (2 * q, q, False), (3 * q, e, False), (3 * q + e, e, True)]


def moe_kernel(
    n, x_hbm, ids_hbm, probs_hbm, flag_hbm, wg_hbm, wu_hbm, wd_hbm, out_hbm,
    tok, ids_v, probs_v, flag_s, tab, wg, wu, wd, acc_g, acc_u, hid, share, part, r1, r2, r3, outv,
    z_send, z_recv, zz_send, zz_recv, y_send, y_recv, s_send, s_recv,
    r1_send, r1_recv, r2_send, r2_recv, r3_send, r3_recv, w_sem, in_sem, out_sem,
):
    nz = n // 4
    steps, rows, width = x_hbm.shape
    ranges = column_units(width)
    per = len(ranges)
    units = steps * per
    me = lax.axis_index("expert")
    k = lax.rem(me, 2)
    y = lax.rem(lax.div(me, 2), 2)
    z = lax.div(me, 4)
    ok, oy = 1 - k, 1 - y
    low, high = z == 0, z == nz - 1
    relay = (z == 1) | (z == nz - 2)
    far = jnp.where(z == 1, nz - 1, 0)

    def zat(d):
        return lax.rem(z + d + nz, nz)

    def nearest(j):
        up = jnp.where(j < z, j, j + 1)
        down = jnp.where(nz - 1 - j > z, nz - 1 - j, nz - 2 - j)
        return jnp.where(z < nz // 2, up, down)

    def dev(zz, yy, kk):
        return {"expert": zz * 4 + yy * 2 + kk}

    def remote(src, dst, ss, rs, target):
        return pltpu.make_async_remote_copy(
            src_ref=src, dst_ref=dst, send_sem=ss, recv_sem=rs,
            device_id=target, device_id_type=MESH,
        )

    sib = dev(z, y, ok)
    ynb = dev(z, oy, k)

    barrier = pltpu.get_barrier_semaphore()
    peers = [sib, ynb] + [dev(zat(d), y, k) for d in range(1, nz)]
    for peer in peers:
        pl.semaphore_signal(barrier, inc=1, device_id=peer, device_id_type=MESH)

    small = [
        pltpu.make_async_copy(ids_hbm, ids_v, in_sem.at[0]),
        pltpu.make_async_copy(probs_hbm, probs_v, in_sem.at[1]),
        pltpu.make_async_copy(flag_hbm, flag_s, in_sem.at[2]),
    ]
    own = pltpu.make_async_copy(x_hbm, tok.at[:, k, y, z, :, pl.ds(0, width)], in_sem.at[3])
    for copy in small + [own]:
        copy.start()
    wcopies = {}
    for c, (lo, size, _) in enumerate(ranges):
        cc = pl.ds(lo, size)
        wcopies["g", c] = pltpu.make_async_copy(wg_hbm.at[0, cc], wg.at[cc], w_sem.at[0, c])
        wcopies["u", c] = pltpu.make_async_copy(wu_hbm.at[0, cc], wu.at[cc], w_sem.at[1, c])
        wcopies["d", c] = pltpu.make_async_copy(wd_hbm.at[0, :, cc], wd.at[:, cc], w_sem.at[2, c])
    for c in range(per):
        wcopies["g", c].start()
        wcopies["u", c].start()
    for c in range(per):
        wcopies["d", c].start()

    tab[...] = jnp.zeros_like(tab)
    for copy in small:
        copy.wait()
    slot = lax.broadcasted_iota(jnp.int32, (n, rows), 0)
    flags = jnp.zeros((n, rows), jnp.int32)
    for e in range(n):
        flags = jnp.where(slot == e, flag_s[e], flags)
    for s in range(steps):
        served = slot if s == 0 else jnp.where(flags == 1, jnp.bitwise_xor(slot, 1), slot)
        ids, probs = ids_v[s], probs_v[s]
        shares = probs / jnp.sum(probs, axis=0, keepdims=True)
        table = jnp.zeros((n, rows), F32)
        for j in range(ids.shape[0]):
            table = jnp.where(ids[j : j + 1] == served, shares[j : j + 1], table)
        coarse = table.astype(BF16).astype(F32)
        tab[2 * s * n : (2 * s + 1) * n, 0:rows] = coarse
        tab[(2 * s + 1) * n : (2 * s + 2) * n, 0:rows] = table - coarse
    tok[0, k, y, z, :, width : width + LANES] = jnp.transpose(tab[...])[0:rows].astype(BF16)
    own.wait()
    pl.semaphore_wait(barrier, len(peers))

    sends = []

    def send(copy, cond=None):
        if cond is None:
            copy.start()
        else:
            pl.when(cond)(copy.start)
        sends.append((copy, cond))

    def spot(u):
        s, c = u // per, u % per
        lo, size, crossed = ranges[c]
        return s, c, pl.ds(lo, size), size, crossed

    def carried(u):
        s, c = u // per, u % per
        lo, size, crossed = ranges[c]
        last = s == 0 and lo + size == width
        return s, pl.ds(lo, size + LANES if last else size), crossed

    def block(u, kk, yy, zz):
        s, cc, _ = carried(u)
        return tok.at[s, kk, yy, zz, :, cc]

    def column(u, kk, yy):
        s, cc, _ = carried(u)
        return tok.at[s, kk, yy, :, :, cc]

    def along_z(u, yy, ss, rs):
        here = block(u, k, yy, z)
        for j in range(nz - 1):
            zz = nearest(j)
            skipped = (low & (zz == nz - 1)) | (high & (zz == 0))
            send(remote(here, here, ss.at[u, zz], rs.at[u, z], dev(zz, y, k)), jnp.logical_not(skipped))

    def arrive_z(u, yy, zs, ss, rs):
        here = block(u, k, yy, zs)
        remote(here, here, ss.at[u, zs], rs.at[u, zs], sib).wait_recv()
        passed = ((z == nz - 2) & (zs == 0)) | ((z == 1) & (zs == nz - 1))
        send(remote(here, here, ss.at[u, z], rs.at[u, zs], dev(nz - 1 - far, y, k)), passed)

    def across_y(u, zz):
        here = block(u, k, y, zz)
        send(remote(here, here, y_send.at[u, zz], y_recv.at[u, zz], ynb))

    def arrive_y(u, zz):
        here = block(u, k, oy, zz)
        remote(here, here, y_send.at[u, zz], y_recv.at[u, zz], ynb).wait_recv()

    def to_sib(u, i, yy):
        col = column(u, k, yy)
        send(remote(col, col, s_send.at[u, i], s_recv.at[u, i], sib))

    def issue(u):
        if carried(u)[2]:
            across_y(u, z)
            along_z(u, y, z_send, z_recv)
        else:
            along_z(u, y, z_send, z_recv)
            across_y(u, z)

    def crossed_on(u):
        arrive_y(u, z)
        along_z(u, oy, zz_send, zz_recv)

    def forward(u):
        crossed = carried(u)[2]
        for j in range(nz - 1):
            zs = nearest(j)
            arrive_z(u, y, zs, z_send, z_recv)
            if not crossed:
                across_y(u, zs)
        to_sib(u, 0, y)

    def forward_other(u):
        crossed = carried(u)[2]
        if not crossed:
            arrive_y(u, z)
        for j in range(nz - 1):
            zs = nearest(j)
            if crossed:
                arrive_z(u, oy, zs, zz_send, zz_recv)
            else:
                arrive_y(u, zs)
        to_sib(u, 1, oy)

    def gathered(u):
        for i, yy in enumerate((y, oy)):
            col = column(u, ok, yy)
            remote(col, col, s_send.at[u, i], s_recv.at[u, i], sib).wait_recv()

    def gate_up(u):
        s, c, cc, size, _ = spot(u)
        if s == 0:
            wcopies["g", c].wait()
            wcopies["u", c].wait()
        lhs = tok[s, :, :, :, :, cc].reshape(n * rows, size)
        g = jnp.dot(lhs, wg[cc, :], preferred_element_type=F32)
        up = jnp.dot(lhs, wu[cc, :], preferred_element_type=F32)
        if c > 0:
            g = acc_g[...] + g
            up = acc_u[...] + up
        if c < per - 1:
            acc_g[...] = g
            acc_u[...] = up
        else:
            hid[...] = (g / (1.0 + jnp.exp(-g)) * up).astype(BF16)
            if s == 0:
                all_shares()

    def all_shares():
        table = tok[0, :, :, :, :, width : width + LANES].reshape(n * rows, LANES).astype(F32)
        lane = lax.broadcasted_iota(jnp.int32, (n * rows, LANES), 1)
        for s in range(steps):
            mine = (lane == 2 * s * n + me) | (lane == (2 * s + 1) * n + me)
            total = jnp.sum(jnp.where(mine, table, 0.0), axis=1, keepdims=True)
            share[s] = jnp.broadcast_to(total, (n * rows, LANES))

    def down(u):
        s, c, cc, size, _ = spot(u)
        if s == 0:
            wcopies["d", c].wait()
        res = jnp.dot(hid[...], wd[:, cc], preferred_element_type=F32)
        part[s, :, :, :, :, cc] = (res * share[s][:, 0:1]).astype(BF16).reshape(2, 2, nz, rows, size)
        send(remote(part.at[s, ok, :, :, :, cc], r1.at[s, :, :, :, cc], r1_send.at[u], r1_recv.at[u], sib))

    def add(*terms):
        total = terms[0].astype(F32)
        for term in terms[1:]:
            total = total + term.astype(F32)
        return total

    def z_back(u, yi, yy, zz):
        s, _, cc, _, _ = spot(u)
        relayed = (low & (zz == nz - 1)) | (high & (zz == 0))
        target = jnp.where(relayed, jnp.where(low, 1, nz - 2), zz)
        place = jnp.where(relayed, target, z)
        return remote(
            part.at[s, k, yy, zz, :, cc], r3.at[s, yi, place, :, cc],
            r3_send.at[u, yi, zz], r3_recv.at[u, yi, place], dev(target, y, k),
        )

    def z_back_all(u, yi, yy):
        for j in range(nz - 1):
            zz = nearest(j)
            later = relay & (zz == far)
            send(z_back(u, yi, yy, zz), jnp.logical_not(later))

    def z_pass(u):
        s, _, cc, _, crossed = spot(u)

        @pl.when(relay)
        def _():
            for yi, yy in enumerate((y, oy) if crossed else (y,)):
                here = r3.at[s, yi, z, :, cc]
                remote(here, here, r3_send.at[u, yi, z], r3_recv.at[u, yi, z], sib).wait_recv()
                part[s, k, yy, far, :, cc] = add(part[s, k, yy, far, :, cc], r3[s, yi, z, :, cc]).astype(BF16)
                z_back(u, yi, yy, far).start()

        for yi, yy in enumerate((y, oy) if crossed else (y,)):
            sends.append((z_back(u, yi, yy, far), relay))

    def z_total(u, yi, yy):
        s, _, cc, _, _ = spot(u)
        terms = [part[s, k, yy, z, :, cc]]
        for j in range(nz - 1):
            zs = nearest(j)
            here = r3.at[s, yi, zs, :, cc]
            copy = remote(here, here, r3_send.at[u, yi, zs], r3_recv.at[u, yi, zs], sib)
            pl.when(jnp.logical_not((low & (zs == nz - 1)) | (high & (zs == 0))))(copy.wait_recv)
            terms.append(r3[s, yi, zs, :, cc])
        return add(*terms)

    def y_back(u):
        s, _, cc, _, crossed = spot(u)
        if crossed:
            src, dst = part.at[s, k, oy, z, :, cc], r2.at[s, z, :, cc]
        else:
            src, dst = part.at[s, k, oy, :, :, cc], r2.at[s, :, :, cc]
        return remote(src, dst, r2_send.at[u], r2_recv.at[u], ynb)

    def rs2(u):
        s, _, cc, _, crossed = spot(u)
        here = r1.at[s, :, :, :, cc]
        remote(here, here, r1_send.at[u], r1_recv.at[u], sib).wait_recv()
        part[s, k, oy, :, :, cc] = add(part[s, k, oy, :, :, cc], r1[s, oy, :, :, cc]).astype(BF16)
        if not crossed:
            send(y_back(u))
        if crossed:
            part[s, k, y, :, :, cc] = add(part[s, k, y, :, :, cc], r1[s, y, :, :, cc]).astype(BF16)
            z_back_all(u, 0, y)
            z_back_all(u, 1, oy)

    def rs3(u):
        s, _, cc, _, crossed = spot(u)
        if not crossed:
            y_back(u).wait_recv()
            part[s, k, y, :, :, cc] = add(
                part[s, k, y, :, :, cc], r1[s, y, :, :, cc], r2[s, :, :, cc]
            ).astype(BF16)
            z_back_all(u, 0, y)
        else:
            z_pass(u)

    def rs4(u):
        s, _, cc, _, crossed = spot(u)
        if not crossed:
            z_pass(u)
        else:
            part[s, k, oy, z, :, cc] = z_total(u, 1, oy).astype(BF16)
            send(y_back(u))

    def rs5(u):
        s, c, cc, _, crossed = spot(u)
        total = z_total(u, 0, y)
        if crossed:
            y_back(u).wait_recv()
            total = total + r2[s, z, :, cc].astype(F32)
        outv[s, :, cc] = total.astype(BF16)
        pltpu.make_async_copy(outv.at[s, :, cc], out_hbm.at[s, :, cc], out_sem.at[s, c]).start()

    @pl.when(low | high)
    def _():
        for s in range(steps):
            for yi in range(2):
                r3[s, yi, nz - 1 - z] = jnp.zeros((rows, width), BF16)

    cross = per - 1
    for u in (cross, *range(per - 1)):
        issue(u)
    crossed_on(cross)

    first = {"down": per + 1, "rs2": per + 2, "rs3": per + 4}
    after = {}
    order = (cross, *range(per - 1))
    for i, c in enumerate(order):
        after.setdefault(first["down"] + i // 2, []).append((down, c))
        after.setdefault(first["rs2"] + i // 2, []).append((rs2, c))
    for t in range(units + 2):
        if t < units:
            forward(t)
            if t + per < units:
                if t == 1:
                    issue(units - 1)
                if t >= 1:
                    issue(t - 1 + per)
                if t == per - 1:
                    crossed_on(units - 1)
        if 0 <= t - 1 < units:
            forward_other(t - 1)
        if t >= 2:
            gathered(t - 2)
            gate_up(t - 2)
        for fn, u in after.get(t, ()):
            fn(u)
    old = list(order)
    new = [per + c for c in order]
    for i in range(per + 4):
        if i < per:
            down(new[i])
        for lag, fn in ((0, rs3), (1, rs4), (3, rs5)):
            if 0 <= i - lag < per:
                fn(old[i - lag])
        if 0 <= i - 1 < per:
            rs2(new[i - 1])
        for lag, fn in ((3, rs3), (4, rs4)):
            if 0 <= i - lag < per:
                fn(new[i - lag])
    for c in new:
        rs5(c)
    for s in range(steps):
        for c, (lo, size, _) in enumerate(ranges):
            cc = pl.ds(lo, size)
            pltpu.make_async_copy(outv.at[s, :, cc], out_hbm.at[s, :, cc], out_sem.at[s, c]).wait()
    for copy, cond in sends:
        if cond is None:
            copy.wait_send()
        else:
            pl.when(cond)(copy.wait_send)


def moe(n, x, ids, probs, flags, wg, wu, wd):
    steps, rows, width = x.shape
    hidden = wg.shape[2]
    nz = n // 4
    per = len(column_units(width))
    units = steps * per
    vm = pltpu.VMEM
    dma = pltpu.SemaphoreType.DMA
    anyspec = pl.BlockSpec(memory_space=pl.ANY)
    return pl.pallas_call(
        functools.partial(moe_kernel, n),
        out_shape=jax.ShapeDtypeStruct(x.shape, BF16),
        in_specs=[anyspec] * 7,
        out_specs=anyspec,
        scratch_shapes=[
            vm((steps, 2, 2, nz, rows, width + LANES), BF16),
            vm(ids.shape, jnp.int32),
            vm(probs.shape, F32),
            pltpu.SMEM(flags.shape, jnp.int32),
            vm((LANES, LANES), F32),
            vm((width, hidden), BF16),
            vm((width, hidden), BF16),
            vm((hidden, width), BF16),
            vm((n * rows, hidden), F32),
            vm((n * rows, hidden), F32),
            vm((n * rows, hidden), BF16),
            vm((steps, n * rows, LANES), F32),
            vm((steps, 2, 2, nz, rows, width), BF16),
            vm((steps, 2, nz, rows, width), BF16),
            vm((steps, nz, rows, width), BF16),
            vm((steps, 2, nz, rows, width), BF16),
            vm((steps, rows, width), BF16),
            dma((units, nz)), dma((units, nz)),
            dma((units, nz)), dma((units, nz)),
            dma((units, nz)), dma((units, nz)),
            dma((units, 2)), dma((units, 2)),
            dma((units,)), dma((units,)),
            dma((units,)), dma((units,)),
            dma((units, 2, nz)), dma((units, 2, nz)),
            dma((3, per)), dma((4,)), dma((steps, per)),
        ],
        compiler_params=pltpu.CompilerParams(
            collective_id=0, has_side_effects=True, vmem_limit_bytes=67000000
        ),
    )(x, ids, probs, flags, wg, wu, wd)


def on_device(hidden_states, expert_ids, router_probs, swap_flags, w_gate, w_up, w_down):
    n = lax.axis_size("expert")
    ids = jnp.swapaxes(expert_ids, 1, 2)
    probs = jnp.swapaxes(router_probs, 1, 2)
    return moe(n, hidden_states, ids, probs, swap_flags, w_gate, w_up, w_down)


def solution(mesh):
    return jax.shard_map(
        on_device,
        mesh=mesh,
        in_specs=(
            P(None, ("groups", "expert"), None),
            P(None, ("groups", "expert"), None),
            P(None, ("groups", "expert"), None),
            P(),
            P("expert", None, None),
            P("expert", None, None),
            P("expert", None, None),
        ),
        out_specs=P(None, ("groups", "expert"), None),
        check_vma=False,
    )
```

```python
import functools

import jax
import jax.numpy as jnp
from jax import lax
from jax.experimental import pallas as pl
from jax.experimental.pallas import tpu as pltpu
from jax.sharding import PartitionSpec as P

MESH = pl.DeviceIdType.MESH
F32 = jnp.float32
BF16 = jnp.bfloat16
LANES = 128
CHUNKS = 4


def plan(steps, per):
    units = steps * per
    seq = []
    for c in range(per):
        seq += [("z", c), ("y", c)]
    for t in range(units):
        seq.append(("f", t))
        if 1 <= t <= per:
            seq += [("z", t - 1 + per), ("y", t - 1 + per)]
        if t >= 1:
            seq.append(("o", t - 1))
        if 2 <= t <= per + 1:
            seq.append(("g", t - 2))
        if per + 1 <= t < units:
            seq += [("d", 2 * (t - per - 1)), ("d", 2 * (t - per - 1) + 1)] if 2 * (t - per - 1) < per else []
    for c in range(per):
        seq.append(("2", c))
    seq += [("o", units - 1)]
    seq += [("g", per + c) for c in range(per)]
    new = [per + c for c in range(per)]
    seq += [("d", new[0]), ("d", new[1]), ("3", 0), ("2", new[0]), ("d", new[2]), ("2", new[1]), ("3", 1)]
    seq += [("d", new[3]), ("2", new[2]), ("3", 2), ("2", new[3]), ("3", 3), ("5", 0), ("5", 1)]
    seq += [("3", new[0]), ("5", 2), ("3", new[1]), ("5", 3), ("3", new[2]), ("5", new[0])]
    seq += [("3", new[3]), ("5", new[1]), ("5", new[2]), ("5", new[3])]
    return seq


def moe_kernel(
    n, x_hbm, ids_hbm, probs_hbm, flag_hbm, wg_hbm, wu_hbm, wd_hbm, out_hbm,
    tok, ids_v, probs_v, flag_s, tab, wgu, wd, acc_g, acc_u, hid, share, part, r1, r2, r3, outv,
    sent, z_recv, y_recv, s_recv, r1_recv, r2_recv, r3_recv, w_sem, in_sem, out_sem,
):
    nz = n // 4
    steps, rows, width = x_hbm.shape
    per = CHUNKS
    dc = width // per
    units = steps * per
    me = lax.axis_index("expert")
    k = lax.rem(me, 2)
    y = lax.rem(lax.div(me, 2), 2)
    z = lax.div(me, 4)
    ok, oy = 1 - k, 1 - y

    def zat(d):
        return lax.rem(z + d + nz, nz)

    def nearest(j):
        up = jnp.where(j < z, j, j + 1)
        down = jnp.where(nz - 1 - j > z, nz - 1 - j, nz - 2 - j)
        return jnp.where(z < nz // 2, up, down)

    def dev(zz, yy, kk):
        return {"expert": zz * 4 + yy * 2 + kk}

    def remote(src, dst, ss, rs, target):
        return pltpu.make_async_remote_copy(
            src_ref=src, dst_ref=dst, send_sem=ss, recv_sem=rs,
            device_id=target, device_id_type=MESH,
        )

    sib = dev(z, y, ok)
    ynb = dev(z, oy, k)

    barrier = pltpu.get_barrier_semaphore()
    peers = [sib, ynb] + [dev(zat(d), y, k) for d in range(1, nz)]
    for peer in peers:
        pl.semaphore_signal(barrier, inc=1, device_id=peer, device_id_type=MESH)

    small = [
        pltpu.make_async_copy(ids_hbm, ids_v, in_sem.at[0]),
        pltpu.make_async_copy(probs_hbm, probs_v, in_sem.at[1]),
        pltpu.make_async_copy(flag_hbm, flag_s, in_sem.at[2]),
    ]
    own = pltpu.make_async_copy(x_hbm, tok.at[:, k, y, z, :, pl.ds(0, width)], in_sem.at[3])
    for copy in small + [own]:
        copy.start()
    wcopies = []
    for c in range(per):
        cc = pl.ds(c * dc, dc)
        wcopies.append(pltpu.make_async_copy(wg_hbm.at[0, cc], wgu.at[0, cc], w_sem.at[0, c]))
        wcopies.append(pltpu.make_async_copy(wu_hbm.at[0, cc], wgu.at[1, cc], w_sem.at[0, c]))
    for c in range(per):
        cc = pl.ds(c * dc, dc)
        wcopies.append(pltpu.make_async_copy(wd_hbm.at[0, :, cc], wd.at[:, cc], w_sem.at[1, c]))
    for copy in wcopies:
        copy.start()

    tab[...] = jnp.zeros_like(tab)
    for copy in small:
        copy.wait()
    slot = lax.broadcasted_iota(jnp.int32, (n, rows), 0)
    flags = jnp.zeros((n, rows), jnp.int32)
    for e in range(n):
        flags = jnp.where(slot == e, flag_s[e], flags)
    for s in range(steps):
        served = slot if s == 0 else jnp.where(flags == 1, jnp.bitwise_xor(slot, 1), slot)
        ids, probs = ids_v[s], probs_v[s]
        shares = probs / jnp.sum(probs, axis=0, keepdims=True)
        table = jnp.zeros((n, rows), F32)
        for j in range(ids.shape[0]):
            table = jnp.where(ids[j : j + 1] == served, shares[j : j + 1], table)
        coarse = table.astype(BF16).astype(F32)
        tab[2 * s * n : (2 * s + 1) * n, 0:rows] = coarse
        tab[(2 * s + 1) * n : (2 * s + 2) * n, 0:rows] = table - coarse
    tok[0, k, y, z, :, width : width + LANES] = jnp.transpose(tab[...])[0:rows].astype(BF16)
    own.wait()
    pl.semaphore_wait(barrier, len(peers))

    def spot(u):
        s, c = u // per, u % per
        return s, c, pl.ds(c * dc, dc)

    def carried(u):
        s, c = u // per, u % per
        last = s == 0 and c == per - 1
        return s, pl.ds(c * dc, dc + LANES if last else dc)

    def arrived(ref, sem):
        remote(ref, ref, sem, sem, sib).wait_recv()

    def block(u, kk, yy, zz):
        s, cc = carried(u)
        return tok.at[s, kk, yy, zz, :, cc]

    def column(u, kk, yy):
        s, cc = carried(u)
        return tok.at[s, kk, yy, :, :, cc]

    def issue_z(u):
        here = block(u, k, y, z)
        for j in range(nz - 1):
            remote(here, here, sent.at[0, u // per], z_recv.at[u, z], dev(nearest(j), y, k)).start()

    def across_y(u, zz):
        here = block(u, k, y, zz)
        remote(here, here, sent.at[1, u // per], y_recv.at[u], ynb).start()

    def issue_y(u):
        across_y(u, z)

    def to_sib(u, yy):
        col = column(u, k, yy)
        remote(col, col, sent.at[2, u // per], s_recv.at[u], sib).start()

    def forward(u):
        for j in range(nz - 1):
            zs = nearest(j)
            arrived(block(u, k, y, zs), z_recv.at[u, zs])
            across_y(u, zs)
        to_sib(u, y)

    def forward_other(u):
        arrived(column(u, k, oy), y_recv.at[u])
        to_sib(u, oy)

    def gate_up(u):
        s, c, cc = spot(u)
        _, wide = carried(u)
        arrived(tok.at[s, ok, :, :, :, wide], s_recv.at[u])
        if s == 0:
            pltpu.make_async_copy(wgu.at[:, cc], wgu.at[:, cc], w_sem.at[0, c]).wait()
        lhs = tok[s, :, :, :, :, cc].reshape(n * rows, dc)
        g = jnp.dot(lhs, wgu[0, cc, :], preferred_element_type=F32)
        up = jnp.dot(lhs, wgu[1, cc, :], preferred_element_type=F32)
        if c > 0:
            g = acc_g[...] + g
            up = acc_u[...] + up
        if c < per - 1:
            acc_g[...] = g
            acc_u[...] = up
        else:
            hid[...] = (g / (1.0 + jnp.exp(-g)) * up).astype(BF16)
            if s == 0:
                all_shares()

    def all_shares():
        table = tok[0, :, :, :, :, width : width + LANES].reshape(n * rows, LANES).astype(F32)
        lane = lax.broadcasted_iota(jnp.int32, (n * rows, LANES), 1)
        for s in range(steps):
            mine = (lane == 2 * s * n + me) | (lane == (2 * s + 1) * n + me)
            total = jnp.sum(jnp.where(mine, table, 0.0), axis=1, keepdims=True)
            share[s] = jnp.broadcast_to(total, (n * rows, LANES))

    def down(u):
        s, c, cc = spot(u)
        if s == 0:
            pltpu.make_async_copy(wd.at[:, cc], wd.at[:, cc], w_sem.at[1, c]).wait()
        res = jnp.dot(hid[...], wd[:, cc], preferred_element_type=F32)
        part[s, :, :, :, :, cc] = (res * share[s][:, 0:1]).astype(BF16).reshape(2, 2, nz, rows, dc)
        remote(part.at[s, ok, :, :, :, cc], r1.at[s, :, :, :, cc], sent.at[3, s], r1_recv.at[u], sib).start()

    def add(*terms):
        total = terms[0].astype(F32)
        for term in terms[1:]:
            total = total + term.astype(F32)
        return total

    def return_y(u):
        s, _, cc = spot(u)
        arrived(r1.at[s, :, :, :, cc], r1_recv.at[u])
        part[s, k, oy, :, :, cc] = add(part[s, k, oy, :, :, cc], r1[s, oy, :, :, cc]).astype(BF16)
        remote(part.at[s, k, oy, :, :, cc], r2.at[s, :, :, cc], sent.at[4, s], r2_recv.at[u], ynb).start()

    def return_z(u):
        s, _, cc = spot(u)
        arrived(r2.at[s, :, :, cc], r2_recv.at[u])
        part[s, k, y, :, :, cc] = add(
            part[s, k, y, :, :, cc], r1[s, y, :, :, cc], r2[s, :, :, cc]
        ).astype(BF16)
        for j in range(nz - 1):
            zz = nearest(j)
            place = jnp.where(z < zz, z, z - 1)
            remote(
                part.at[s, k, y, zz, :, cc], r3.at[s, place, :, cc],
                sent.at[5, s], r3_recv.at[u], dev(zz, y, k),
            ).start()

    def finish(u):
        s, c, cc = spot(u)
        arrived(r3.at[s, :, :, cc], r3_recv.at[u])
        total = add(part[s, k, y, z, :, cc], *(r3[s, d, :, cc] for d in range(nz - 1)))
        outv[s, :, cc] = total.astype(BF16)
        pltpu.make_async_copy(outv.at[s, :, cc], out_hbm.at[s, :, cc], out_sem).start()

    stages = {
        "y": issue_y, "z": issue_z, "f": forward, "o": forward_other, "g": gate_up,
        "d": down, "2": return_y, "3": return_z, "5": finish,
    }
    for name, u in plan(steps, per):
        stages[name](u)

    for s in range(steps):
        cols = pl.ds(0, width + LANES if s == 0 else width)
        done = [
            tok.at[s, 0, 0, pl.ds(0, nz - 1), :, cols], tok.at[s, 0, 0, :, :, cols], tok.at[s, 0, :, :, :, cols],
            r1.at[s], r2.at[s], r3.at[s],
        ]
        for kind, ref in enumerate(done):
            remote(ref, ref, sent.at[kind, s], sent.at[kind, s], sib).wait_send()
    pltpu.make_async_copy(outv, outv, out_sem).wait()


def moe(n, x, ids, probs, flags, wg, wu, wd):
    steps, rows, width = x.shape
    hidden = wg.shape[2]
    nz = n // 4
    per = CHUNKS
    units = steps * per
    vm = pltpu.VMEM
    dma = pltpu.SemaphoreType.DMA
    anyspec = pl.BlockSpec(memory_space=pl.ANY)
    return pl.pallas_call(
        functools.partial(moe_kernel, n),
        out_shape=jax.ShapeDtypeStruct(x.shape, BF16),
        in_specs=[anyspec] * 7,
        out_specs=anyspec,
        scratch_shapes=[
            vm((steps, 2, 2, nz, rows, width + LANES), BF16),
            vm(ids.shape, jnp.int32),
            vm(probs.shape, F32),
            pltpu.SMEM(flags.shape, jnp.int32),
            vm((LANES, LANES), F32),
            vm((2, width, hidden), BF16),
            vm((hidden, width), BF16),
            vm((n * rows, hidden), F32),
            vm((n * rows, hidden), F32),
            vm((n * rows, hidden), BF16),
            vm((steps, n * rows, LANES), F32),
            vm((steps, 2, 2, nz, rows, width), BF16),
            vm((steps, 2, nz, rows, width), BF16),
            vm((steps, nz, rows, width), BF16),
            vm((steps, nz - 1, rows, width), BF16),
            vm((steps, rows, width), BF16),
            dma((6, steps)), dma((units, nz)), dma((units,)), dma((units,)),
            dma((units,)), dma((units,)), dma((units,)), dma((2, per)), dma((4,)), dma,
        ],
        compiler_params=pltpu.CompilerParams(
            collective_id=0, has_side_effects=True, vmem_limit_bytes=67000000
        ),
    )(x, ids, probs, flags, wg, wu, wd)


def on_device(hidden_states, expert_ids, router_probs, swap_flags, w_gate, w_up, w_down):
    n = lax.axis_size("expert")
    ids = jnp.swapaxes(expert_ids, 1, 2)
    probs = jnp.swapaxes(router_probs, 1, 2)
    return moe(n, hidden_states, ids, probs, swap_flags, w_gate, w_up, w_down)


def solution(mesh):
    return jax.shard_map(
        on_device,
        mesh=mesh,
        in_specs=(
            P(None, ("groups", "expert"), None),
            P(None, ("groups", "expert"), None),
            P(None, ("groups", "expert"), None),
            P(),
            P("expert", None, None),
            P("expert", None, None),
            P("expert", None, None),
        ),
        out_specs=P(None, ("groups", "expert"), None),
        check_vma=False,
    )
```

```python
import functools

import jax
import jax.numpy as jnp
from jax import lax
from jax.experimental import pallas as pl
from jax.experimental.pallas import tpu as pltpu
from jax.sharding import PartitionSpec as P

MESH = pl.DeviceIdType.MESH
F32 = jnp.float32
BF16 = jnp.bfloat16
LANES = 128
RELAY = True
EIGHTHS = (2, 2, 2, 2)
GATHER_CROSSED = (1, 1)
RETURN_CROSSED = (0, 0)


def plan(steps, per):
    units = steps * per
    gather, back = [], []
    for s in range(steps):
        first, rest = range(GATHER_CROSSED[s]), range(GATHER_CROSSED[s], per)
        gather.append([s * per + c for c in (*rest, *first)])
        first, rest = range(RETURN_CROSSED[s]), range(RETURN_CROSSED[s], per)
        back.append([s * per + c for c in (*first, *rest)])
    seq = []
    for s in range(steps):
        seq += [("y", u) for u in gather[s][per - GATHER_CROSSED[s] :] + gather[s][: per - GATHER_CROSSED[s]]]
        if s == 0:
            seq += [("z", u) for u in gather[0]]
    order = gather[0] + gather[1]
    lag = 3
    half = back[0][: (per + 1) // 2]
    for t in range(units + 1):
        if t < units:
            seq.append(("f", order[t]))
        if 1 <= t <= per:
            seq.append(("z", order[t - 1 + per]))
        if 1 <= t:
            seq.append(("F", order[t - 1]))
        if 2 <= t:
            seq.append(("o", order[t - 2]))
        if lag <= t < per + lag:
            seq.append(("g", order[t - lag]))
        if t == per + lag - 1:
            seq += [("d", u) for u in half]
        if t == per + lag:
            seq += [("d", u) for u in back[0] if u not in half]
    seq += [("2", u) for u in back[0]]
    seq.append(("o", order[units - 1]))
    seq += [("g", u) for u in gather[1]]
    old, new = list(back[0]), list(back[1])
    seq += [("d", new[0]), ("d", new[1]), ("3", old[0]), ("2", new[0])]
    for c in range(2, per):
        seq += [("d", new[c]), ("2", new[c - 1]), ("3", old[c - 1])]
    seq += [("2", new[per - 1]), ("3", old[per - 1])]
    seq += [("5", old[0]), ("5", old[1])]
    for c in range(per):
        seq += [("3", new[c])] + [("5", u) for u in old[c + 2 : c + 3]] + ([("5", new[c - 2])] if c >= 2 else [])
    seq += [("5", u) for u in new[per - 2 :]]
    return seq


def moe_kernel(
    n, x_hbm, ids_hbm, probs_hbm, flag_hbm, wg_hbm, wu_hbm, wd_hbm, out_hbm,
    tok, ids_v, probs_v, flag_s, tab, wgu, wd, acc_g, acc_u, hid, share, part, r1, r2, r3, outv,
    sent, z_recv, zx_recv, y_recv, s_recv, r1_recv, r2_recv, r3_recv, rx_recv, w_sem, in_sem, out_sem,
):
    nz = n // 4
    steps, rows, width = x_hbm.shape
    per = len(EIGHTHS)
    sizes = [part_of * width // 8 for part_of in EIGHTHS]
    lows = [sum(sizes[:c]) for c in range(per + 1)]
    units = steps * per
    me = lax.axis_index("expert")
    k = lax.rem(me, 2)
    y = lax.rem(lax.div(me, 2), 2)
    z = lax.div(me, 4)
    ok, oy = 1 - k, 1 - y
    low, high = z == 0, z == nz - 1
    relay = (z == 1) | (z == nz - 2)

    def zat(d):
        return lax.rem(z + d + nz, nz)

    def nearest(j):
        up = jnp.where(j < z, j, j + 1)
        down = jnp.where(nz - 1 - j > z, nz - 1 - j, nz - 2 - j)
        return jnp.where(z < nz // 2, up, down)

    def source(j):
        return jnp.where(relay, nearest((j + nz - 2) % (nz - 1)), nearest(j)) if RELAY else nearest(j)

    def dev(zz, yy, kk):
        return {"expert": zz * 4 + yy * 2 + kk}

    def remote(src, dst, ss, rs, target):
        return pltpu.make_async_remote_copy(
            src_ref=src, dst_ref=dst, send_sem=ss, recv_sem=rs,
            device_id=target, device_id_type=MESH,
        )

    sib = dev(z, y, ok)
    ynb = dev(z, oy, k)

    barrier = pltpu.get_barrier_semaphore()
    peers = [sib, ynb] + [dev(zat(d), y, k) for d in range(1, nz)]
    for peer in peers:
        pl.semaphore_signal(barrier, inc=1, device_id=peer, device_id_type=MESH)

    small = [
        pltpu.make_async_copy(ids_hbm, ids_v, in_sem.at[0]),
        pltpu.make_async_copy(probs_hbm, probs_v, in_sem.at[1]),
        pltpu.make_async_copy(flag_hbm, flag_s, in_sem.at[2]),
    ]
    own = pltpu.make_async_copy(x_hbm, tok.at[:, k, y, z, :, pl.ds(0, width)], in_sem.at[3])
    for copy in small + [own]:
        copy.start()
    wcopies = []
    for c in range(per):
        cc = pl.ds(lows[c], sizes[c])
        wcopies.append(pltpu.make_async_copy(wg_hbm.at[0, cc], wgu.at[0, cc], w_sem.at[0, c]))
        wcopies.append(pltpu.make_async_copy(wu_hbm.at[0, cc], wgu.at[1, cc], w_sem.at[0, c]))
    for c in range(per):
        cc = pl.ds(lows[c], sizes[c])
        wcopies.append(pltpu.make_async_copy(wd_hbm.at[0, :, cc], wd.at[:, cc], w_sem.at[1, c]))
    for copy in wcopies:
        copy.start()

    tab[...] = jnp.zeros_like(tab)
    for copy in small:
        copy.wait()
    slot = lax.broadcasted_iota(jnp.int32, (n, rows), 0)
    flags = jnp.zeros((n, rows), jnp.int32)
    for e in range(n):
        flags = jnp.where(slot == e, flag_s[e], flags)
    for s in range(steps):
        served = slot if s == 0 else jnp.where(flags == 1, jnp.bitwise_xor(slot, 1), slot)
        ids, probs = ids_v[s], probs_v[s]
        shares = probs / jnp.sum(probs, axis=0, keepdims=True)
        table = jnp.zeros((n, rows), F32)
        for j in range(ids.shape[0]):
            table = jnp.where(ids[j : j + 1] == served, shares[j : j + 1], table)
        coarse = table.astype(BF16).astype(F32)
        tab[2 * s * n : (2 * s + 1) * n, 0:rows] = coarse
        tab[(2 * s + 1) * n : (2 * s + 2) * n, 0:rows] = table - coarse
    tok[0, k, y, z, :, width : width + LANES] = jnp.transpose(tab[...])[0:rows].astype(BF16)
    own.wait()
    pl.semaphore_wait(barrier, len(peers))

    def spot(u):
        s, c = u // per, u % per
        return s, c, pl.ds(lows[c], sizes[c])

    def carried(u):
        s, c = u // per, u % per
        last = s == 0 and c == per - 1
        return s, pl.ds(lows[c], sizes[c] + LANES if last else sizes[c]), c < GATHER_CROSSED[s]

    def arrived(ref, sem):
        remote(ref, ref, sem, sem, sib).wait_recv()

    def block(u, kk, yy, zz):
        s, cc, _ = carried(u)
        return tok.at[s, kk, yy, zz, :, cc]

    def column(u, kk, yy):
        s, cc, _ = carried(u)
        return tok.at[s, kk, yy, :, :, cc]

    def along_z(u, yy, kind, recv):
        here = block(u, k, yy, z)
        for j in range(nz - 1):
            zz = source(j)
            copy = remote(here, here, sent.at[kind, u // per], recv.at[u, z], dev(zz, y, k))
            if RELAY:
                pl.when(jnp.logical_not((low & (zz == nz - 1)) | (high & (zz == 0))))(copy.start)
            else:
                copy.start()

    def issue_z(u):
        s, _, crossed = carried(u)
        along_z(u, y, 6 if crossed else 0, z_recv)
        if crossed:
            arrived(block(u, k, oy, z), y_recv.at[u])
            along_z(u, oy, 6, zx_recv)

    def across_y(u, zz):
        here = block(u, k, y, zz)
        remote(here, here, sent.at[7 if carried(u)[2] else 1, u // per], y_recv.at[u], ynb).start()

    def issue_y(u):
        across_y(u, z)

    def arrive_z(u, yy, zs, kind, recv):
        here = block(u, k, yy, zs)
        arrived(here, recv.at[u, zs])
        if RELAY:
            passed = ((z == nz - 2) & (zs == 0)) | ((z == 1) & (zs == nz - 1))
            onward = dev(jnp.where(z == 1, 0, nz - 1), y, k)
            pl.when(passed)(remote(here, here, sent.at[kind, u // per], recv.at[u, zs], onward).start)

    def forward_from(u, j):
        crossed = carried(u)[2]
        zs = source(j)
        if crossed:
            arrive_z(u, y, zs, 6, z_recv)
            arrive_z(u, oy, zs, 6, zx_recv)
        else:
            arrive_z(u, y, zs, 0, z_recv)
            across_y(u, zs)

    def forward(u):
        for j in range(nz - 2):
            forward_from(u, j)

    def forward_last(u):
        s, cc, crossed = carried(u)
        forward_from(u, nz - 2)
        if crossed:
            both = tok.at[s, k, :, :, :, cc]
            remote(both, both, sent.at[2, s], s_recv.at[u], sib).start()
        else:
            col = column(u, k, y)
            remote(col, col, sent.at[2, s], s_recv.at[u], sib).start()

    def forward_other(u):
        s, _, crossed = carried(u)
        if not crossed:
            col = column(u, k, oy)
            arrived(col, y_recv.at[u])
            remote(col, col, sent.at[2, s], s_recv.at[u], sib).start()

    def gate_up(u):
        s, c, cc = spot(u)
        _, wide, _ = carried(u)
        arrived(tok.at[s, ok, :, :, :, wide], s_recv.at[u])
        if s == 0:
            pltpu.make_async_copy(wgu.at[:, cc], wgu.at[:, cc], w_sem.at[0, c]).wait()
        lhs = tok[s, :, :, :, :, cc].reshape(n * rows, sizes[c])
        g = jnp.dot(lhs, wgu[0, cc, :], preferred_element_type=F32)
        up = jnp.dot(lhs, wgu[1, cc, :], preferred_element_type=F32)
        first = GATHER_CROSSED[s] % per
        if c != first:
            g = acc_g[...] + g
            up = acc_u[...] + up
        if c != (first - 1) % per:
            acc_g[...] = g
            acc_u[...] = up
        else:
            hid[...] = (g / (1.0 + jnp.exp(-g)) * up).astype(BF16)
            if s == 0:
                all_shares()

    def all_shares():
        table = tok[0, :, :, :, :, width : width + LANES].reshape(n * rows, LANES).astype(F32)
        lane = lax.broadcasted_iota(jnp.int32, (n * rows, LANES), 1)
        for s in range(steps):
            mine = (lane == 2 * s * n + me) | (lane == (2 * s + 1) * n + me)
            total = jnp.sum(jnp.where(mine, table, 0.0), axis=1, keepdims=True)
            share[s] = jnp.broadcast_to(total, (n * rows, LANES))

    def down(u):
        s, c, cc = spot(u)
        if s == 0:
            pltpu.make_async_copy(wd.at[:, cc], wd.at[:, cc], w_sem.at[1, c]).wait()
        res = jnp.dot(hid[...], wd[:, cc], preferred_element_type=F32)
        part[s, :, :, :, :, cc] = (res * share[s][:, 0:1]).astype(BF16).reshape(2, 2, nz, rows, sizes[c])
        remote(part.at[s, ok, :, :, :, cc], r1.at[s, :, :, :, cc], sent.at[3, s], r1_recv.at[u], sib).start()

    def add(*terms):
        total = terms[0].astype(F32)
        for term in terms[1:]:
            total = total + term.astype(F32)
        return total

    def back_z(u, yi, yy, kind, recv):
        s, _, cc = spot(u)
        for j in range(nz - 1):
            zz = nearest(j)
            place = jnp.where(z < zz, z, z - 1)
            remote(
                part.at[s, k, yy, zz, :, cc], r3.at[s, yi, place, :, cc],
                sent.at[kind, s], recv.at[u], dev(zz, y, k),
            ).start()

    def total_z(u, yi, yy, recv):
        s, _, cc = spot(u)
        arrived(r3.at[s, yi, :, :, cc], recv.at[u])
        return add(part[s, k, yy, z, :, cc], *(r3[s, yi, d, :, cc] for d in range(nz - 1)))

    def return_first(u):
        s, c, cc = spot(u)
        arrived(r1.at[s, :, :, :, cc], r1_recv.at[u])
        part[s, k, oy, :, :, cc] = add(part[s, k, oy, :, :, cc], r1[s, oy, :, :, cc]).astype(BF16)
        if c < RETURN_CROSSED[s]:
            back_z(u, 1, oy, 8, rx_recv)
            part[s, k, y, :, :, cc] = add(part[s, k, y, :, :, cc], r1[s, y, :, :, cc]).astype(BF16)
            back_z(u, 0, y, 8, r3_recv)
        else:
            remote(part.at[s, k, oy, :, :, cc], r2.at[s, :, :, cc], sent.at[4, s], r2_recv.at[u], ynb).start()

    def return_second(u):
        s, c, cc = spot(u)
        if c < RETURN_CROSSED[s]:
            part[s, k, oy, z, :, cc] = total_z(u, 1, oy, rx_recv).astype(BF16)
            remote(part.at[s, k, oy, z, :, cc], r2.at[s, 0, :, cc], sent.at[9, s], r2_recv.at[u], ynb).start()
        else:
            arrived(r2.at[s, :, :, cc], r2_recv.at[u])
            part[s, k, y, :, :, cc] = add(
                part[s, k, y, :, :, cc], r1[s, y, :, :, cc], r2[s, :, :, cc]
            ).astype(BF16)
            back_z(u, 0, y, 5, r3_recv)

    def finish(u):
        s, c, cc = spot(u)
        total = total_z(u, 0, y, r3_recv)
        if c < RETURN_CROSSED[s]:
            arrived(r2.at[s, 0, :, cc], r2_recv.at[u])
            total = total + r2[s, 0, :, cc].astype(F32)
        outv[s, :, cc] = total.astype(BF16)
        pltpu.make_async_copy(outv.at[s, :, cc], out_hbm.at[s, :, cc], out_sem).start()

    stages = {
        "y": issue_y, "z": issue_z, "f": forward, "F": forward_last, "o": forward_other, "g": gate_up,
        "d": down, "2": return_first, "3": return_second, "5": finish,
    }
    for name, u in plan(steps, per):
        stages[name](u)

    def all_sent(kind, s, ref):
        remote(ref, ref, sent.at[kind, s], sent.at[kind, s], sib).wait_send()

    for s in range(steps):
        extra = LANES if s == 0 else 0
        split = lows[GATHER_CROSSED[s]]
        crossed, straight = pl.ds(0, split), pl.ds(split, width + extra - split)
        counts = [(None, nz - 1)]
        if RELAY:
            ends = low | high
            counts = [(ends, nz - 2), (relay, nz)]
            if nz > 4:
                counts.append((jnp.logical_not(ends | relay), nz - 1))
        for cond, count in counts:
            def sent_z(s=s, count=count, crossed=crossed, straight=straight, split=split):
                all_sent(0, s, tok.at[s, 0, 0, pl.ds(0, count), :, straight])
                if split:
                    all_sent(6, s, tok.at[s, 0, :, pl.ds(0, count), :, crossed])
            if cond is None:
                sent_z()
            else:
                pl.when(cond)(sent_z)
        all_sent(1, s, tok.at[s, 0, 0, :, :, straight])
        if split:
            all_sent(7, s, tok.at[s, 0, 0, 0, :, crossed])
        all_sent(2, s, tok.at[s, 0, :, :, :, pl.ds(0, width + extra)])
        all_sent(3, s, r1.at[s])
        split = lows[RETURN_CROSSED[s]]
        crossed, straight = pl.ds(0, split), pl.ds(split, width - split)
        all_sent(4, s, r2.at[s, :, :, straight])
        all_sent(5, s, r3.at[s, 0, :, :, straight])
        if split:
            all_sent(8, s, r3.at[s, :, :, :, crossed])
            all_sent(9, s, r2.at[s, 0, :, crossed])
    pltpu.make_async_copy(outv, outv, out_sem).wait()


def moe(n, x, ids, probs, flags, wg, wu, wd):
    steps, rows, width = x.shape
    hidden = wg.shape[2]
    nz = n // 4
    per = len(EIGHTHS)
    units = steps * per
    vm = pltpu.VMEM
    dma = pltpu.SemaphoreType.DMA
    anyspec = pl.BlockSpec(memory_space=pl.ANY)
    return pl.pallas_call(
        functools.partial(moe_kernel, n),
        out_shape=jax.ShapeDtypeStruct(x.shape, BF16),
        in_specs=[anyspec] * 7,
        out_specs=anyspec,
        scratch_shapes=[
            vm((steps, 2, 2, nz, rows, width + LANES), BF16),
            vm(ids.shape, jnp.int32),
            vm(probs.shape, F32),
            pltpu.SMEM(flags.shape, jnp.int32),
            vm((LANES, LANES), F32),
            vm((2, width, hidden), BF16),
            vm((hidden, width), BF16),
            vm((n * rows, hidden), F32),
            vm((n * rows, hidden), F32),
            vm((n * rows, hidden), BF16),
            vm((steps, n * rows, LANES), F32),
            vm((steps, 2, 2, nz, rows, width), BF16),
            vm((steps, 2, nz, rows, width), BF16),
            vm((steps, nz, rows, width), BF16),
            vm((steps, 2, nz - 1, rows, width), BF16),
            vm((steps, rows, width), BF16),
            dma((10, steps)), dma((units, nz)), dma((units, nz)), dma((units,)), dma((units,)),
            dma((units,)), dma((units,)), dma((units,)), dma((units,)), dma((2, per)), dma((4,)), dma,
        ],
        compiler_params=pltpu.CompilerParams(
            collective_id=0, has_side_effects=True, vmem_limit_bytes=67000000
        ),
    )(x, ids, probs, flags, wg, wu, wd)


def on_device(hidden_states, expert_ids, router_probs, swap_flags, w_gate, w_up, w_down):
    n = lax.axis_size("expert")
    ids = jnp.swapaxes(expert_ids, 1, 2)
    probs = jnp.swapaxes(router_probs, 1, 2)
    return moe(n, hidden_states, ids, probs, swap_flags, w_gate, w_up, w_down)


def solution(mesh):
    return jax.shard_map(
        on_device,
        mesh=mesh,
        in_specs=(
            P(None, ("groups", "expert"), None),
            P(None, ("groups", "expert"), None),
            P(None, ("groups", "expert"), None),
            P(),
            P("expert", None, None),
            P("expert", None, None),
            P("expert", None, None),
        ),
        out_specs=P(None, ("groups", "expert"), None),
        check_vma=False,
    )
```

```python
import functools

import jax
import jax.numpy as jnp
from jax import lax
from jax.experimental import pallas as pl
from jax.experimental.pallas import tpu as pltpu
from jax.sharding import PartitionSpec as P

MESH = pl.DeviceIdType.MESH
F32 = jnp.float32
BF16 = jnp.bfloat16
LANES = 128
RELAY = True
EIGHTHS = (2, 2, 2, 2)
GATHER_CROSSED = (1, 1)
RETURN_CROSSED = (1, 0)
RETURN_RELAY = (False, False)
LAG, OLAG = 3, 2
AHEAD, YOWN = 3, 1


def plan(steps, per):
    units = steps * per
    gather, back = [], []
    for s in range(steps):
        first, rest = range(GATHER_CROSSED[s]), range(GATHER_CROSSED[s], per)
        gather.append([s * per + c for c in (*rest, *first)])
        first, rest = range(RETURN_CROSSED[s]), range(RETURN_CROSSED[s], per)
        back.append([s * per + c for c in (*first, *rest)])
    old, new = back
    seq = []
    order = gather[0] + gather[1]
    own = [gather[s][per - GATHER_CROSSED[s] :] + gather[s][: per - GATHER_CROSSED[s]] for s in range(steps)]
    lag = LAG
    seq += [("y", u) for u in own[0]]
    seq += [("z", u) for u in order[:AHEAD]]
    for t in range(units):
        if t == YOWN:
            seq += [("y", u) for u in own[1]]
        seq.append(("f", order[t]))
        if t + AHEAD < units and (t > 0 or AHEAD < per):
            seq.append(("z", order[t + AHEAD]))
        if 1 <= t:
            seq.append(("F", order[t - 1]))
        if OLAG <= t:
            seq.append(("o", order[t - OLAG]))
        if lag <= t < per + lag:
            seq.append(("g", order[t - lag]))
        if t == per + lag - 1:
            seq += [("d", u) for u in old[:2]]
    seq += [("g", order[t - lag]) for t in range(units, per + lag)]
    if per + lag - 1 >= units:
        seq += [("d", u) for u in old[:2]]
    seq += [("2", old[0]), ("2", old[1])]
    seq += [("d", u) for u in old[2:]]
    seq += [("F", order[units - 1])]
    seq += [("2", u) for u in old[2:]]
    seq += [("o", order[t]) for t in range(units - OLAG, units)]
    seq += [("g", u) for u in gather[1]]
    a, b, c, d = old
    e, f, g, h = new
    if RETURN_CROSSED[0]:
        a, b, c, d = b, c, a, d
    seq += [("d", e), ("d", f), ("3", a), ("2", e), ("d", g), ("2", f), ("3", b), ("p", a)]
    seq += [("d", h), ("2", g), ("3", c), ("p", b), ("2", h), ("3", d), ("p", c), ("5", a), ("p", d)]
    seq += [("3", e), ("5", b), ("3", f), ("5", c), ("3", g), ("5", d), ("5", e)]
    seq += [("3", h), ("5", f), ("5", g), ("5", h)]
    return seq


def moe_kernel(
    n, x_hbm, ids_hbm, probs_hbm, flag_hbm, wg_hbm, wu_hbm, wd_hbm, out_hbm,
    tok, ids_v, probs_v, flag_s, tab, wgu, wd, acc_g, acc_u, hid, share, part, r1, r2, r3, outv,
    sent, z_recv, zx_recv, y_recv, s_recv, r1_recv, r2_recv, r3_recv, rx_recv, w_sem, in_sem, out_sem,
):
    nz = n // 4
    steps, rows, width = x_hbm.shape
    per = len(EIGHTHS)
    sizes = [part_of * width // 8 for part_of in EIGHTHS]
    lows = [sum(sizes[:c]) for c in range(per + 1)]
    units = steps * per
    me = lax.axis_index("expert")
    k = lax.rem(me, 2)
    y = lax.rem(lax.div(me, 2), 2)
    z = lax.div(me, 4)
    ok, oy = 1 - k, 1 - y
    low, high = z == 0, z == nz - 1
    relay = (z == 1) | (z == nz - 2)

    def zat(d):
        return lax.rem(z + d + nz, nz)

    def nearest(j):
        up = jnp.where(j < z, j, j + 1)
        down = jnp.where(nz - 1 - j > z, nz - 1 - j, nz - 2 - j)
        return jnp.where(z < nz // 2, up, down)

    def source(j):
        return jnp.where(relay, nearest((j + nz - 2) % (nz - 1)), nearest(j)) if RELAY else nearest(j)

    def dev(zz, yy, kk):
        return {"expert": zz * 4 + yy * 2 + kk}

    def remote(src, dst, ss, rs, target):
        return pltpu.make_async_remote_copy(
            src_ref=src, dst_ref=dst, send_sem=ss, recv_sem=rs,
            device_id=target, device_id_type=MESH,
        )

    sib = dev(z, y, ok)
    ynb = dev(z, oy, k)

    barrier = pltpu.get_barrier_semaphore()
    peers = [sib, ynb] + [dev(zat(d), y, k) for d in range(1, nz)]
    for peer in peers:
        pl.semaphore_signal(barrier, inc=1, device_id=peer, device_id_type=MESH)

    small = [
        pltpu.make_async_copy(ids_hbm, ids_v, in_sem.at[0]),
        pltpu.make_async_copy(probs_hbm, probs_v, in_sem.at[1]),
        pltpu.make_async_copy(flag_hbm, flag_s, in_sem.at[2]),
    ]
    own = pltpu.make_async_copy(x_hbm, tok.at[:, k, y, z, :, pl.ds(0, width)], in_sem.at[3])
    for copy in small + [own]:
        copy.start()
    wcopies = []
    for c in range(per):
        cc = pl.ds(lows[c], sizes[c])
        wcopies.append(pltpu.make_async_copy(wg_hbm.at[0, cc], wgu.at[0, cc], w_sem.at[0, c]))
        wcopies.append(pltpu.make_async_copy(wu_hbm.at[0, cc], wgu.at[1, cc], w_sem.at[0, c]))
    for c in range(per):
        cc = pl.ds(lows[c], sizes[c])
        wcopies.append(pltpu.make_async_copy(wd_hbm.at[0, :, cc], wd.at[:, cc], w_sem.at[1, c]))
    for copy in wcopies:
        copy.start()

    tab[...] = jnp.zeros_like(tab)
    for copy in small:
        copy.wait()
    slot = lax.broadcasted_iota(jnp.int32, (n, rows), 0)
    flags = jnp.zeros((n, rows), jnp.int32)
    for e in range(n):
        flags = jnp.where(slot == e, flag_s[e], flags)
    for s in range(steps):
        served = slot if s == 0 else jnp.where(flags == 1, jnp.bitwise_xor(slot, 1), slot)
        ids, probs = ids_v[s], probs_v[s]
        shares = probs / jnp.sum(probs, axis=0, keepdims=True)
        table = jnp.zeros((n, rows), F32)
        for j in range(ids.shape[0]):
            table = jnp.where(ids[j : j + 1] == served, shares[j : j + 1], table)
        coarse = table.astype(BF16).astype(F32)
        tab[2 * s * n : (2 * s + 1) * n, 0:rows] = coarse
        tab[(2 * s + 1) * n : (2 * s + 2) * n, 0:rows] = table - coarse
    tok[0, k, y, z, :, width : width + LANES] = jnp.transpose(tab[...])[0:rows].astype(BF16)
    own.wait()
    pl.semaphore_wait(barrier, len(peers))

    def spot(u):
        s, c = u // per, u % per
        return s, c, pl.ds(lows[c], sizes[c])

    def carried(u):
        s, c = u // per, u % per
        last = s == 0 and c == per - 1
        return s, pl.ds(lows[c], sizes[c] + LANES if last else sizes[c]), c < GATHER_CROSSED[s]

    def arrived(ref, sem):
        remote(ref, ref, sem, sem, sib).wait_recv()

    def block(u, kk, yy, zz):
        s, cc, _ = carried(u)
        return tok.at[s, kk, yy, zz, :, cc]

    def column(u, kk, yy):
        s, cc, _ = carried(u)
        return tok.at[s, kk, yy, :, :, cc]

    def along_z(u, yy, kind, recv):
        here = block(u, k, yy, z)
        for j in range(nz - 1):
            zz = source(j)
            copy = remote(here, here, sent.at[kind, u // per], recv.at[u, z], dev(zz, y, k))
            if RELAY:
                pl.when(jnp.logical_not((low & (zz == nz - 1)) | (high & (zz == 0))))(copy.start)
            else:
                copy.start()

    def issue_z(u):
        s, _, crossed = carried(u)
        along_z(u, y, 6 if crossed else 0, z_recv)
        if crossed:
            arrived(block(u, k, oy, z), y_recv.at[u])
            along_z(u, oy, 6, zx_recv)

    def across_y(u, zz):
        here = block(u, k, y, zz)
        remote(here, here, sent.at[7 if carried(u)[2] else 1, u // per], y_recv.at[u], ynb).start()

    def issue_y(u):
        across_y(u, z)

    def arrive_z(u, yy, zs, kind, recv):
        here = block(u, k, yy, zs)
        arrived(here, recv.at[u, zs])
        if RELAY:
            passed = ((z == nz - 2) & (zs == 0)) | ((z == 1) & (zs == nz - 1))
            onward = dev(jnp.where(z == 1, 0, nz - 1), y, k)
            pl.when(passed)(remote(here, here, sent.at[kind, u // per], recv.at[u, zs], onward).start)

    def forward_from(u, j):
        crossed = carried(u)[2]
        zs = source(j)
        if crossed:
            arrive_z(u, y, zs, 6, z_recv)
            arrive_z(u, oy, zs, 6, zx_recv)
        else:
            arrive_z(u, y, zs, 0, z_recv)
            across_y(u, zs)

    def forward(u):
        for j in range(nz - 2):
            forward_from(u, j)

    def forward_last(u):
        s, cc, crossed = carried(u)
        forward_from(u, nz - 2)
        if crossed:
            both = tok.at[s, k, :, :, :, cc]
            remote(both, both, sent.at[2, s], s_recv.at[u], sib).start()
        else:
            col = column(u, k, y)
            remote(col, col, sent.at[2, s], s_recv.at[u], sib).start()

    def forward_other(u):
        s, _, crossed = carried(u)
        if not crossed:
            col = column(u, k, oy)
            arrived(col, y_recv.at[u])
            remote(col, col, sent.at[2, s], s_recv.at[u], sib).start()

    def gate_up(u):
        s, c, cc = spot(u)
        _, wide, _ = carried(u)
        arrived(tok.at[s, ok, :, :, :, wide], s_recv.at[u])
        if s == 0:
            pltpu.make_async_copy(wgu.at[:, cc], wgu.at[:, cc], w_sem.at[0, c]).wait()
        lhs = tok[s, :, :, :, :, cc].reshape(n * rows, sizes[c])
        g = jnp.dot(lhs, wgu[0, cc, :], preferred_element_type=F32)
        up = jnp.dot(lhs, wgu[1, cc, :], preferred_element_type=F32)
        first = GATHER_CROSSED[s] % per
        if c != first:
            g = acc_g[...] + g
            up = acc_u[...] + up
        if c != (first - 1) % per:
            acc_g[...] = g
            acc_u[...] = up
        else:
            hid[...] = (g / (1.0 + jnp.exp(-g)) * up).astype(BF16)
            if s == 0:
                all_shares()

    def all_shares():
        table = tok[0, :, :, :, :, width : width + LANES].reshape(n * rows, LANES).astype(F32)
        lane = lax.broadcasted_iota(jnp.int32, (n * rows, LANES), 1)
        for s in range(steps):
            mine = (lane == 2 * s * n + me) | (lane == (2 * s + 1) * n + me)
            total = jnp.sum(jnp.where(mine, table, 0.0), axis=1, keepdims=True)
            share[s] = jnp.broadcast_to(total, (n * rows, LANES))

    def down(u):
        s, c, cc = spot(u)
        if s == 0:
            pltpu.make_async_copy(wd.at[:, cc], wd.at[:, cc], w_sem.at[1, c]).wait()
        res = jnp.dot(hid[...], wd[:, cc], preferred_element_type=F32)
        part[s, :, :, :, :, cc] = (res * share[s][:, 0:1]).astype(BF16).reshape(2, 2, nz, rows, sizes[c])
        remote(part.at[s, ok, :, :, :, cc], r1.at[s, :, :, :, cc], sent.at[3, s], r1_recv.at[u], sib).start()

    def add(*terms):
        total = terms[0].astype(F32)
        for term in terms[1:]:
            total = total + term.astype(F32)
        return total

    ends = low | high
    far = jnp.where(z == 1, nz - 1, 0)

    def back_copy(u, yi, yy, zz, kind, recv):
        s, _, cc = spot(u)
        relayed = ends & (zz == nz - 1 - z) if RETURN_RELAY[s] else False
        place = jnp.where(relayed, nz - 1, jnp.where(z < zz, z, z - 1))
        target = jnp.where(relayed, jnp.where(low, 1, nz - 2), zz)
        return remote(
            part.at[s, k, yy, zz, :, cc], r3.at[s, yi, place, :, cc],
            sent.at[kind, s], recv.at[u, jnp.where(relayed, 1, 0)], dev(target, y, k),
        )

    def back_z(u, yi, yy, kind, recv):
        for j in range(nz - 1):
            zz = nearest(j)
            copy = back_copy(u, yi, yy, zz, kind, recv)
            if RETURN_RELAY[u // per]:
                pl.when(jnp.logical_not(relay & (zz == far)))(copy.start)
            else:
                copy.start()

    def relay_z(u):
        s, c, cc = spot(u)
        if not RETURN_RELAY[s]:
            return

        @pl.when(relay)
        def _():
            if c < RETURN_CROSSED[s]:
                ways = ((1, oy, 8, rx_recv), (0, y, 8, r3_recv))
            else:
                ways = ((0, y, 5, r3_recv),)
            for yi, yy, kind, recv in ways:
                arrived(r3.at[s, yi, nz - 1, :, cc], recv.at[u, 1])
                part[s, k, yy, far, :, cc] = add(part[s, k, yy, far, :, cc], r3[s, yi, nz - 1, :, cc]).astype(BF16)
                back_copy(u, yi, yy, far, kind, recv).start()

    def total_z(u, yi, yy, recv):
        s, _, cc = spot(u)
        if RETURN_RELAY[s]:
            pl.when(ends)(lambda: arrived(r3.at[s, yi, pl.ds(0, nz - 2), :, cc], recv.at[u, 0]))
            pl.when(jnp.logical_not(ends))(lambda: arrived(r3.at[s, yi, pl.ds(0, nz - 1), :, cc], recv.at[u, 0]))
        else:
            arrived(r3.at[s, yi, pl.ds(0, nz - 1), :, cc], recv.at[u, 0])
        return add(part[s, k, yy, z, :, cc], *(r3[s, yi, d, :, cc] for d in range(nz - 1)))

    for s in range(steps):
        if RETURN_RELAY[s]:
            @pl.when(ends)
            def _(s=s):
                for yi in range(2):
                    r3[s, yi, jnp.where(low, nz - 2, 0)] = jnp.zeros((rows, width), BF16)

    def return_first(u):
        s, c, cc = spot(u)
        arrived(r1.at[s, :, :, :, cc], r1_recv.at[u])
        part[s, k, oy, :, :, cc] = add(part[s, k, oy, :, :, cc], r1[s, oy, :, :, cc]).astype(BF16)
        if c < RETURN_CROSSED[s]:
            back_z(u, 1, oy, 8, rx_recv)
            part[s, k, y, :, :, cc] = add(part[s, k, y, :, :, cc], r1[s, y, :, :, cc]).astype(BF16)
            back_z(u, 0, y, 8, r3_recv)
        else:
            remote(part.at[s, k, oy, :, :, cc], r2.at[s, :, :, cc], sent.at[4, s], r2_recv.at[u], ynb).start()

    def return_second(u):
        s, c, cc = spot(u)
        if c < RETURN_CROSSED[s]:
            part[s, k, oy, z, :, cc] = total_z(u, 1, oy, rx_recv).astype(BF16)
            remote(part.at[s, k, oy, z, :, cc], r2.at[s, 0, :, cc], sent.at[9, s], r2_recv.at[u], ynb).start()
        else:
            arrived(r2.at[s, :, :, cc], r2_recv.at[u])
            part[s, k, y, :, :, cc] = add(
                part[s, k, y, :, :, cc], r1[s, y, :, :, cc], r2[s, :, :, cc]
            ).astype(BF16)
            back_z(u, 0, y, 5, r3_recv)

    def finish(u):
        s, c, cc = spot(u)
        total = total_z(u, 0, y, r3_recv)
        if c < RETURN_CROSSED[s]:
            arrived(r2.at[s, 0, :, cc], r2_recv.at[u])
            total = total + r2[s, 0, :, cc].astype(F32)
        outv[s, :, cc] = total.astype(BF16)
        pltpu.make_async_copy(outv.at[s, :, cc], out_hbm.at[s, :, cc], out_sem).start()

    stages = {
        "y": issue_y, "z": issue_z, "f": forward, "F": forward_last, "o": forward_other, "g": gate_up,
        "d": down, "2": return_first, "3": return_second, "p": relay_z, "5": finish,
    }
    for name, u in plan(steps, per):
        stages[name](u)

    def all_sent(kind, s, ref):
        remote(ref, ref, sent.at[kind, s], sent.at[kind, s], sib).wait_send()

    for s in range(steps):
        extra = LANES if s == 0 else 0
        split = lows[GATHER_CROSSED[s]]
        crossed, straight = pl.ds(0, split), pl.ds(split, width + extra - split)
        counts = [(None, nz - 1)]
        if RELAY:
            counts = [(ends, nz - 2), (relay, nz)]
            if nz > 4:
                counts.append((jnp.logical_not(ends | relay), nz - 1))
        for cond, count in counts:
            def sent_z(s=s, count=count, crossed=crossed, straight=straight, split=split):
                all_sent(0, s, tok.at[s, 0, 0, pl.ds(0, count), :, straight])
                if split:
                    all_sent(6, s, tok.at[s, 0, :, pl.ds(0, count), :, crossed])
            if cond is None:
                sent_z()
            else:
                pl.when(cond)(sent_z)
        all_sent(1, s, tok.at[s, 0, 0, :, :, straight])
        if split:
            all_sent(7, s, tok.at[s, 0, 0, 0, :, crossed])
        all_sent(2, s, tok.at[s, 0, :, :, :, pl.ds(0, width + extra)])
        all_sent(3, s, r1.at[s])
        split = lows[RETURN_CROSSED[s]]
        crossed, straight = pl.ds(0, split), pl.ds(split, width - split)
        all_sent(4, s, r2.at[s, :, :, straight])
        all_sent(5, s, r3.at[s, 0, pl.ds(0, nz - 1), :, straight])
        if split:
            all_sent(8, s, r3.at[s, :, pl.ds(0, nz - 1), :, crossed])
            all_sent(9, s, r2.at[s, 0, :, crossed])
    pltpu.make_async_copy(outv, outv, out_sem).wait()


def moe(n, x, ids, probs, flags, wg, wu, wd):
    steps, rows, width = x.shape
    hidden = wg.shape[2]
    nz = n // 4
    per = len(EIGHTHS)
    units = steps * per
    vm = pltpu.VMEM
    dma = pltpu.SemaphoreType.DMA
    anyspec = pl.BlockSpec(memory_space=pl.ANY)
    return pl.pallas_call(
        functools.partial(moe_kernel, n),
        out_shape=jax.ShapeDtypeStruct(x.shape, BF16),
        in_specs=[anyspec] * 7,
        out_specs=anyspec,
        scratch_shapes=[
            vm((steps, 2, 2, nz, rows, width + LANES), BF16),
            vm(ids.shape, jnp.int32),
            vm(probs.shape, F32),
            pltpu.SMEM(flags.shape, jnp.int32),
            vm((LANES, LANES), F32),
            vm((2, width, hidden), BF16),
            vm((hidden, width), BF16),
            vm((n * rows, hidden), F32),
            vm((n * rows, hidden), F32),
            vm((n * rows, hidden), BF16),
            vm((steps, n * rows, LANES), F32),
            vm((steps, 2, 2, nz, rows, width), BF16),
            vm((steps, 2, nz, rows, width), BF16),
            vm((steps, nz, rows, width), BF16),
            vm((steps, 2, nz, rows, width), BF16),
            vm((steps, rows, width), BF16),
            dma((10, steps)), dma((units, nz)), dma((units, nz)), dma((units,)), dma((units,)),
            dma((units,)), dma((units,)), dma((units, 2)), dma((units, 2)), dma((2, per)), dma((4,)), dma,
        ],
        compiler_params=pltpu.CompilerParams(
            collective_id=0, has_side_effects=True, vmem_limit_bytes=67000000
        ),
    )(x, ids, probs, flags, wg, wu, wd)


def on_device(hidden_states, expert_ids, router_probs, swap_flags, w_gate, w_up, w_down):
    n = lax.axis_size("expert")
    ids = jnp.swapaxes(expert_ids, 1, 2)
    probs = jnp.swapaxes(router_probs, 1, 2)
    return moe(n, hidden_states, ids, probs, swap_flags, w_gate, w_up, w_down)


def solution(mesh):
    return jax.shard_map(
        on_device,
        mesh=mesh,
        in_specs=(
            P(None, ("groups", "expert"), None),
            P(None, ("groups", "expert"), None),
            P(None, ("groups", "expert"), None),
            P(),
            P("expert", None, None),
            P("expert", None, None),
            P("expert", None, None),
        ),
        out_specs=P(None, ("groups", "expert"), None),
        check_vma=False,
    )
```

```python
import functools

import jax
import jax.numpy as jnp
from jax import lax
from jax.experimental import pallas as pl
from jax.experimental.pallas import tpu as pltpu
from jax.sharding import PartitionSpec as P

MESH = pl.DeviceIdType.MESH
F32 = jnp.float32
BF16 = jnp.bfloat16
LANES = 128
RELAY = True
EIGHTHS = (2, 2, 2, 2)
GATHER_CROSSED = (1, 1)
RETURN_CROSSED = (1, 0)
LAG, OLAG = 3, 2
AHEAD, YOWN = 3, 1


def plan(steps, per):
    units = steps * per
    gather, back = [], []
    for s in range(steps):
        first, rest = range(GATHER_CROSSED[s]), range(GATHER_CROSSED[s], per)
        gather.append([s * per + c for c in (*rest, *first)])
        first, rest = range(RETURN_CROSSED[s]), range(RETURN_CROSSED[s], per)
        back.append([s * per + c for c in (*first, *rest)])
    old, new = back
    seq = []
    order = gather[0] + gather[1]
    own = [gather[s][per - GATHER_CROSSED[s] :] + gather[s][: per - GATHER_CROSSED[s]] for s in range(steps)]
    lag = LAG
    seq += [("y", u) for u in own[0]]
    seq += [("z", u) for u in order[:AHEAD]]
    for t in range(units):
        if t == YOWN:
            seq += [("y", u) for u in own[1]]
        seq.append(("f", order[t]))
        if t + AHEAD < units and (t > 0 or AHEAD < per):
            seq.append(("z", order[t + AHEAD]))
        if t == per + lag - 1:
            seq.append(("g", order[per - 1]))
            seq += [("d", u) for u in old[:2]]
        if 1 <= t:
            seq.append(("F", order[t - 1]))
        if OLAG <= t:
            seq.append(("o", order[t - OLAG]))
        if lag <= t < per + lag - 1:
            seq.append(("g", order[t - lag]))
    seq += [("2", old[0]), ("2", old[1])]
    seq += [("d", u) for u in old[2:]]
    seq += [("F", order[units - 1])]
    seq += [("2", u) for u in old[2:]]
    seq += [("o", order[t]) for t in range(units - OLAG, units)]
    a, b, c, d = old
    e, f, g, h = new
    if RETURN_CROSSED[0]:
        a, b, c, d = b, c, a, d
    last = gather[1]
    seq += [("g", last[0]), ("g", last[1]), ("g", last[2]), ("3", a), ("g", last[3]), ("d", e), ("d", f), ("3", b)]
    seq += [("2", e), ("d", g), ("2", f), ("d", h), ("2", g), ("3", d), ("2", h), ("3", c), ("5", a)]
    seq += [("3", e), ("5", b), ("3", f), ("5", d), ("3", g), ("5", c), ("5", e)]
    seq += [("3", h), ("5", f), ("5", g), ("5", h)]
    return seq


def moe_kernel(
    n, x_hbm, ids_hbm, probs_hbm, flag_hbm, wg_hbm, wu_hbm, wd_hbm, out_hbm,
    tok, ids_v, probs_v, flag_s, tab, wgu, wd, acc_g, acc_u, hid, share, part, r1, r2, r3, outv,
    sent, z_recv, zx_recv, y_recv, s_recv, r1_recv, r2_recv, r3_recv, rx_recv, w_sem, in_sem, out_sem,
):
    nz = n // 4
    steps, rows, width = x_hbm.shape
    per = len(EIGHTHS)
    sizes = [part_of * width // 8 for part_of in EIGHTHS]
    lows = [sum(sizes[:c]) for c in range(per + 1)]
    units = steps * per
    me = lax.axis_index("expert")
    k = lax.rem(me, 2)
    y = lax.rem(lax.div(me, 2), 2)
    z = lax.div(me, 4)
    ok, oy = 1 - k, 1 - y
    low, high = z == 0, z == nz - 1
    relay = (z == 1) | (z == nz - 2)

    def zat(d):
        return lax.rem(z + d + nz, nz)

    def nearest(j):
        up = jnp.where(j < z, j, j + 1)
        down = jnp.where(nz - 1 - j > z, nz - 1 - j, nz - 2 - j)
        return jnp.where(z < nz // 2, up, down)

    def source(j):
        return jnp.where(relay, nearest((j + nz - 2) % (nz - 1)), nearest(j)) if RELAY else nearest(j)

    def dev(zz, yy, kk):
        return {"expert": zz * 4 + yy * 2 + kk}

    def remote(src, dst, ss, rs, target):
        return pltpu.make_async_remote_copy(
            src_ref=src, dst_ref=dst, send_sem=ss, recv_sem=rs,
            device_id=target, device_id_type=MESH,
        )

    sib = dev(z, y, ok)
    ynb = dev(z, oy, k)

    barrier = pltpu.get_barrier_semaphore()
    peers = [sib, ynb] + [dev(zat(d), y, k) for d in range(1, nz)]
    for peer in peers:
        pl.semaphore_signal(barrier, inc=1, device_id=peer, device_id_type=MESH)

    small = [
        pltpu.make_async_copy(ids_hbm, ids_v, in_sem.at[0]),
        pltpu.make_async_copy(probs_hbm, probs_v, in_sem.at[1]),
        pltpu.make_async_copy(flag_hbm, flag_s, in_sem.at[2]),
    ]
    own = pltpu.make_async_copy(x_hbm, tok.at[:, k, y, z, :, pl.ds(0, width)], in_sem.at[3])
    for copy in small + [own]:
        copy.start()
    wcopies = []
    for c in range(per):
        cc = pl.ds(lows[c], sizes[c])
        wcopies.append(pltpu.make_async_copy(wg_hbm.at[0, cc], wgu.at[0, cc], w_sem.at[0, c]))
        wcopies.append(pltpu.make_async_copy(wu_hbm.at[0, cc], wgu.at[1, cc], w_sem.at[0, c]))
    for c in range(per):
        cc = pl.ds(lows[c], sizes[c])
        wcopies.append(pltpu.make_async_copy(wd_hbm.at[0, :, cc], wd.at[:, cc], w_sem.at[1, c]))
    for copy in wcopies:
        copy.start()

    tab[...] = jnp.zeros_like(tab)
    for copy in small:
        copy.wait()
    slot = lax.broadcasted_iota(jnp.int32, (n, rows), 0)
    flags = jnp.zeros((n, rows), jnp.int32)
    for e in range(n):
        flags = jnp.where(slot == e, flag_s[e], flags)
    for s in range(steps):
        served = slot if s == 0 else jnp.where(flags == 1, jnp.bitwise_xor(slot, 1), slot)
        ids, probs = ids_v[s], probs_v[s]
        shares = probs / jnp.sum(probs, axis=0, keepdims=True)
        table = jnp.zeros((n, rows), F32)
        for j in range(ids.shape[0]):
            table = jnp.where(ids[j : j + 1] == served, shares[j : j + 1], table)
        coarse = table.astype(BF16).astype(F32)
        tab[2 * s * n : (2 * s + 1) * n, 0:rows] = coarse
        tab[(2 * s + 1) * n : (2 * s + 2) * n, 0:rows] = table - coarse
    tok[0, k, y, z, :, width : width + LANES] = jnp.transpose(tab[...])[0:rows].astype(BF16)
    own.wait()
    pl.semaphore_wait(barrier, len(peers))

    def spot(u):
        s, c = u // per, u % per
        return s, c, pl.ds(lows[c], sizes[c])

    def carried(u):
        s, c = u // per, u % per
        last = s == 0 and c == per - 1
        return s, pl.ds(lows[c], sizes[c] + LANES if last else sizes[c]), c < GATHER_CROSSED[s]

    def extra_of(u):
        return sum(GATHER_CROSSED[: u // per]) + u % per

    def arrived(ref, sem):
        remote(ref, ref, sem, sem, sib).wait_recv()

    def block(u, kk, yy, zz):
        s, cc, _ = carried(u)
        return tok.at[s, kk, yy, zz, :, cc]

    def column(u, kk, yy):
        s, cc, _ = carried(u)
        return tok.at[s, kk, yy, :, :, cc]

    def along_z(u, yy, kind, recv, at):
        here = block(u, k, yy, z)
        for j in range(nz - 1):
            zz = source(j)
            copy = remote(here, here, sent.at[kind, u // per], recv.at[at, z], dev(zz, y, k))
            if RELAY:
                pl.when(jnp.logical_not((low & (zz == nz - 1)) | (high & (zz == 0))))(copy.start)
            else:
                copy.start()

    def issue_z(u):
        s, _, crossed = carried(u)
        along_z(u, y, 6 if crossed else 0, z_recv, u)
        if crossed:
            arrived(block(u, k, oy, z), y_recv.at[u])
            along_z(u, oy, 6, zx_recv, extra_of(u))

    def across_y(u, zz):
        here = block(u, k, y, zz)
        remote(here, here, sent.at[7 if carried(u)[2] else 1, u // per], y_recv.at[u], ynb).start()

    def issue_y(u):
        across_y(u, z)

    def arrive_z(u, yy, zs, kind, recv, at):
        here = block(u, k, yy, zs)
        arrived(here, recv.at[at, zs])
        if RELAY:
            passed = ((z == nz - 2) & (zs == 0)) | ((z == 1) & (zs == nz - 1))
            onward = dev(jnp.where(z == 1, 0, nz - 1), y, k)
            pl.when(passed)(remote(here, here, sent.at[kind, u // per], recv.at[at, zs], onward).start)

    def forward_from(u, j):
        crossed = carried(u)[2]
        zs = source(j)
        if crossed:
            arrive_z(u, y, zs, 6, z_recv, u)
            arrive_z(u, oy, zs, 6, zx_recv, extra_of(u))
        else:
            arrive_z(u, y, zs, 0, z_recv, u)
            across_y(u, zs)

    def forward(u):
        for j in range(nz - 2):
            forward_from(u, j)

    def forward_last(u):
        s, cc, crossed = carried(u)
        forward_from(u, nz - 2)
        if crossed:
            both = tok.at[s, k, :, :, :, cc]
            remote(both, both, sent.at[2, s], s_recv.at[u], sib).start()
        else:
            col = column(u, k, y)
            remote(col, col, sent.at[2, s], s_recv.at[u], sib).start()

    def forward_other(u):
        s, _, crossed = carried(u)
        if not crossed:
            col = column(u, k, oy)
            arrived(col, y_recv.at[u])
            remote(col, col, sent.at[2, s], s_recv.at[u], sib).start()

    def gate_up(u):
        s, c, cc = spot(u)
        _, wide, _ = carried(u)
        arrived(tok.at[s, ok, :, :, :, wide], s_recv.at[u])
        if s == 0:
            pltpu.make_async_copy(wgu.at[:, cc], wgu.at[:, cc], w_sem.at[0, c]).wait()
        lhs = tok[s, :, :, :, :, cc].reshape(n * rows, sizes[c])
        g = jnp.dot(lhs, wgu[0, cc, :], preferred_element_type=F32)
        up = jnp.dot(lhs, wgu[1, cc, :], preferred_element_type=F32)
        first = GATHER_CROSSED[s] % per
        if c != first:
            g = acc_g[...] + g
            up = acc_u[...] + up
        if c != (first - 1) % per:
            acc_g[...] = g
            acc_u[...] = up
        else:
            hid[...] = (g / (1.0 + jnp.exp(-g)) * up).astype(BF16)
            if s == 0:
                all_shares()

    def all_shares():
        table = tok[0, :, :, :, :, width : width + LANES].reshape(n * rows, LANES).astype(F32)
        lane = lax.broadcasted_iota(jnp.int32, (n * rows, LANES), 1)
        for s in range(steps):
            mine = (lane == 2 * s * n + me) | (lane == (2 * s + 1) * n + me)
            total = jnp.sum(jnp.where(mine, table, 0.0), axis=1, keepdims=True)
            share[s] = jnp.broadcast_to(total, (n * rows, LANES))

    def down(u):
        s, c, cc = spot(u)
        if s == 0:
            pltpu.make_async_copy(wd.at[:, cc], wd.at[:, cc], w_sem.at[1, c]).wait()
        res = jnp.dot(hid[...], wd[:, cc], preferred_element_type=F32)
        part[s, :, :, :, :, cc] = (res * share[s][:, 0:1]).astype(BF16).reshape(2, 2, nz, rows, sizes[c])
        remote(part.at[s, ok, :, :, :, cc], r1.at[s, :, :, :, cc], sent.at[3, s], r1_recv.at[u], sib).start()

    def add(*terms):
        total = terms[0].astype(F32)
        for term in terms[1:]:
            total = total + term.astype(F32)
        return total

    def back_z(u, yi, yy, kind, sem):
        s, _, cc = spot(u)
        for j in range(nz - 1):
            zz = nearest(j)
            place = jnp.where(z < zz, z, z - 1)
            remote(
                part.at[s, k, yy, zz, :, cc], r3.at[s, yi, place, :, cc],
                sent.at[kind, s], sem, dev(zz, y, k),
            ).start()

    def total_z(u, yi, yy, sem):
        s, _, cc = spot(u)
        arrived(r3.at[s, yi, :, :, cc], sem)
        return add(part[s, k, yy, z, :, cc], *(r3[s, yi, d, :, cc] for d in range(nz - 1)))

    def return_first(u):
        s, c, cc = spot(u)
        arrived(r1.at[s, :, :, :, cc], r1_recv.at[u])
        part[s, k, oy, :, :, cc] = add(part[s, k, oy, :, :, cc], r1[s, oy, :, :, cc]).astype(BF16)
        if c < RETURN_CROSSED[s]:
            back_z(u, 1, oy, 8, rx_recv.at[s, c])
            part[s, k, y, :, :, cc] = add(part[s, k, y, :, :, cc], r1[s, y, :, :, cc]).astype(BF16)
            back_z(u, 0, y, 8, r3_recv.at[u])
        else:
            remote(part.at[s, k, oy, :, :, cc], r2.at[s, :, :, cc], sent.at[4, s], r2_recv.at[u], ynb).start()

    def return_second(u):
        s, c, cc = spot(u)
        if c < RETURN_CROSSED[s]:
            part[s, k, oy, z, :, cc] = total_z(u, 1, oy, rx_recv.at[s, c]).astype(BF16)
            remote(part.at[s, k, oy, z, :, cc], r2.at[s, 0, :, cc], sent.at[9, s], r2_recv.at[u], ynb).start()
        else:
            arrived(r2.at[s, :, :, cc], r2_recv.at[u])
            part[s, k, y, :, :, cc] = add(
                part[s, k, y, :, :, cc], r1[s, y, :, :, cc], r2[s, :, :, cc]
            ).astype(BF16)
            back_z(u, 0, y, 5, r3_recv.at[u])

    def finish(u):
        s, c, cc = spot(u)
        total = total_z(u, 0, y, r3_recv.at[u])
        if c < RETURN_CROSSED[s]:
            arrived(r2.at[s, 0, :, cc], r2_recv.at[u])
            total = total + r2[s, 0, :, cc].astype(F32)
        outv[s, :, cc] = total.astype(BF16)
        pltpu.make_async_copy(outv.at[s, :, cc], out_hbm.at[s, :, cc], out_sem).start()

    stages = {
        "y": issue_y, "z": issue_z, "f": forward, "F": forward_last, "o": forward_other, "g": gate_up,
        "d": down, "2": return_first, "3": return_second, "5": finish,
    }
    for name, u in plan(steps, per):
        stages[name](u)

    def all_sent(kind, s, ref):
        remote(ref, ref, sent.at[kind, s], sent.at[kind, s], sib).wait_send()

    for s in range(steps):
        extra = LANES if s == 0 else 0
        split = lows[GATHER_CROSSED[s]]
        crossed, straight = pl.ds(0, split), pl.ds(split, width + extra - split)
        counts = [(None, nz - 1)]
        if RELAY:
            ends = low | high
            counts = [(ends, nz - 2), (relay, nz)]
            if nz > 4:
                counts.append((jnp.logical_not(ends | relay), nz - 1))
        for cond, count in counts:
            def sent_z(s=s, count=count, crossed=crossed, straight=straight, split=split):
                all_sent(0, s, tok.at[s, 0, 0, pl.ds(0, count), :, straight])
                if split:
                    all_sent(6, s, tok.at[s, 0, :, pl.ds(0, count), :, crossed])
            if cond is None:
                sent_z()
            else:
                pl.when(cond)(sent_z)
        all_sent(1, s, tok.at[s, 0, 0, :, :, straight])
        if split:
            all_sent(7, s, tok.at[s, 0, 0, 0, :, crossed])
        all_sent(2, s, tok.at[s, 0, :, :, :, pl.ds(0, width + extra)])
        all_sent(3, s, r1.at[s])
        split = lows[RETURN_CROSSED[s]]
        crossed, straight = pl.ds(0, split), pl.ds(split, width - split)
        all_sent(4, s, r2.at[s, :, :, straight])
        all_sent(5, s, r3.at[s, 0, :, :, straight])
        if split:
            all_sent(8, s, r3.at[s, :, :, :, crossed])
            all_sent(9, s, r2.at[s, 0, :, crossed])
    pltpu.make_async_copy(outv, outv, out_sem).wait()


def moe(n, x, ids, probs, flags, wg, wu, wd):
    steps, rows, width = x.shape
    hidden = wg.shape[2]
    nz = n // 4
    per = len(EIGHTHS)
    units = steps * per
    vm = pltpu.VMEM
    dma = pltpu.SemaphoreType.DMA
    anyspec = pl.BlockSpec(memory_space=pl.ANY)
    return pl.pallas_call(
        functools.partial(moe_kernel, n),
        out_shape=jax.ShapeDtypeStruct(x.shape, BF16),
        in_specs=[anyspec] * 7,
        out_specs=anyspec,
        scratch_shapes=[
            vm((steps, 2, 2, nz, rows, width + LANES), BF16),
            vm(ids.shape, jnp.int32),
            vm(probs.shape, F32),
            pltpu.SMEM(flags.shape, jnp.int32),
            vm((LANES, LANES), F32),
            vm((2, width, hidden), BF16),
            vm((hidden, width), BF16),
            vm((n * rows, hidden), F32),
            vm((n * rows, hidden), F32),
            vm((n * rows, hidden), BF16),
            vm((steps, n * rows, LANES), F32),
            vm((steps, 2, 2, nz, rows, width), BF16),
            vm((steps, 2, nz, rows, width), BF16),
            vm((steps, nz, rows, width), BF16),
            vm((steps, 2, nz - 1, rows, width), BF16),
            vm((steps, rows, width), BF16),
            dma((10, steps)), dma((units, nz)), dma((sum(GATHER_CROSSED), nz)), dma((units,)), dma((units,)),
            dma((units,)), dma((units,)), dma((units,)), dma((steps, max(RETURN_CROSSED))), dma((2, per)), dma((4,)), dma,
        ],
        compiler_params=pltpu.CompilerParams(
            collective_id=0, has_side_effects=True, vmem_limit_bytes=67000000
        ),
    )(x, ids, probs, flags, wg, wu, wd)


def on_device(hidden_states, expert_ids, router_probs, swap_flags, w_gate, w_up, w_down):
    n = lax.axis_size("expert")
    ids = jnp.swapaxes(expert_ids, 1, 2)
    probs = jnp.swapaxes(router_probs, 1, 2)
    return moe(n, hidden_states, ids, probs, swap_flags, w_gate, w_up, w_down)


def solution(mesh):
    return jax.shard_map(
        on_device,
        mesh=mesh,
        in_specs=(
            P(None, ("groups", "expert"), None),
            P(None, ("groups", "expert"), None),
            P(None, ("groups", "expert"), None),
            P(),
            P("expert", None, None),
            P("expert", None, None),
            P("expert", None, None),
        ),
        out_specs=P(None, ("groups", "expert"), None),
        check_vma=False,
    )
```

```python
import functools

import jax
import jax.numpy as jnp
from jax import lax
from jax.experimental import pallas as pl
from jax.experimental.pallas import tpu as pltpu
from jax.sharding import PartitionSpec as P

MESH = pl.DeviceIdType.MESH
F32 = jnp.float32
BF16 = jnp.bfloat16
LANES = 128
RELAY = True
EIGHTHS = (2, 2, 2, 2)
GATHER_CROSSED = (1, 1)
RETURN_CROSSED = (1, 0)
LAG, OLAG = 3, 2
AHEAD, YOWN = 3, 1


def plan(steps, per):
    units = steps * per
    gather, back = [], []
    for s in range(steps):
        first, rest = range(GATHER_CROSSED[s]), range(GATHER_CROSSED[s], per)
        gather.append([s * per + c for c in (*rest, *first)])
        first, rest = range(RETURN_CROSSED[s]), range(RETURN_CROSSED[s], per)
        back.append([s * per + c for c in (*first, *rest)])
    old, new = back
    seq = []
    order = gather[0] + gather[1]
    own = [gather[s][per - GATHER_CROSSED[s] :] + gather[s][: per - GATHER_CROSSED[s]] for s in range(steps)]
    lag = LAG
    seq += [("y", u) for u in own[0]]
    seq += [("z", u) for u in order[:AHEAD]]
    for t in range(units):
        if t == YOWN:
            seq += [("y", u) for u in own[1]]
        seq.append(("f", order[t]))
        if t + AHEAD < units and (t > 0 or AHEAD < per):
            seq.append(("z", order[t + AHEAD]))
        if t == per + lag - 1:
            seq.append(("g", order[per - 1]))
            seq += [("d", u) for u in old[:2]]
        if 1 <= t:
            seq.append(("F", order[t - 1]))
        if t == units - 1:
            seq += [("2", old[0]), ("2", old[1])]
        if OLAG <= t:
            seq.append(("o", order[t - OLAG]))
        if lag <= t < per + lag - 1:
            seq.append(("g", order[t - lag]))
    seq += [("d", u) for u in old[2:]]
    seq += [("F", order[units - 1])]
    seq += [("2", u) for u in old[2:]]
    seq += [("o", order[t]) for t in range(units - OLAG, units)]
    a, b, c, d = old
    e, f, g, h = new
    if RETURN_CROSSED[0]:
        a, b, c, d = b, c, a, d
    last = gather[1]
    seq += [("g", last[0]), ("g", last[1]), ("g", last[2]), ("3", a), ("g", last[3]), ("d", e), ("d", f), ("3", b)]
    seq += [("2", e), ("d", g), ("2", f), ("d", h), ("2", g), ("3", d), ("2", h), ("3", c)]
    seq += [("3", e), ("5", a), ("5", b), ("3", f), ("5", d), ("3", g), ("5", e), ("3", h), ("5", c)]
    seq += [("5", f), ("5", g), ("5", h)]
    return seq


def moe_kernel(
    n, x_hbm, ids_hbm, probs_hbm, flag_hbm, wg_hbm, wu_hbm, wd_hbm, out_hbm,
    tok, ids_v, probs_v, flag_s, tab, wgu, wd, acc_g, acc_u, hid, share, part, r1, r2, r3, outv,
    sent, z_recv, zx_recv, y_recv, s_recv, r1_recv, r2_recv, r3_recv, rx_recv, w_sem, in_sem, out_sem,
):
    nz = n // 4
    steps, rows, width = x_hbm.shape
    per = len(EIGHTHS)
    sizes = [part_of * width // 8 for part_of in EIGHTHS]
    lows = [sum(sizes[:c]) for c in range(per + 1)]
    units = steps * per
    me = lax.axis_index("expert")
    k = lax.rem(me, 2)
    y = lax.rem(lax.div(me, 2), 2)
    z = lax.div(me, 4)
    ok, oy = 1 - k, 1 - y
    low, high = z == 0, z == nz - 1
    relay = (z == 1) | (z == nz - 2)

    def zat(d):
        return lax.rem(z + d + nz, nz)

    def nearest(j):
        up = jnp.where(j < z, j, j + 1)
        down = jnp.where(nz - 1 - j > z, nz - 1 - j, nz - 2 - j)
        return jnp.where(z < nz // 2, up, down)

    def source(j):
        return jnp.where(relay, nearest((j + nz - 2) % (nz - 1)), nearest(j)) if RELAY else nearest(j)

    def dev(zz, yy, kk):
        return {"expert": zz * 4 + yy * 2 + kk}

    def remote(src, dst, ss, rs, target):
        return pltpu.make_async_remote_copy(
            src_ref=src, dst_ref=dst, send_sem=ss, recv_sem=rs,
            device_id=target, device_id_type=MESH,
        )

    sib = dev(z, y, ok)
    ynb = dev(z, oy, k)

    barrier = pltpu.get_barrier_semaphore()
    peers = [sib, ynb] + [dev(zat(d), y, k) for d in range(1, nz)]
    for peer in peers:
        pl.semaphore_signal(barrier, inc=1, device_id=peer, device_id_type=MESH)

    small = [
        pltpu.make_async_copy(ids_hbm, ids_v, in_sem.at[0]),
        pltpu.make_async_copy(probs_hbm, probs_v, in_sem.at[1]),
        pltpu.make_async_copy(flag_hbm, flag_s, in_sem.at[2]),
    ]
    own = pltpu.make_async_copy(x_hbm, tok.at[:, k, y, z, :, pl.ds(0, width)], in_sem.at[3])
    for copy in small + [own]:
        copy.start()
    wcopies = []
    for c in range(per):
        cc = pl.ds(lows[c], sizes[c])
        wcopies.append(pltpu.make_async_copy(wg_hbm.at[0, cc], wgu.at[0, cc], w_sem.at[0, c]))
        wcopies.append(pltpu.make_async_copy(wu_hbm.at[0, cc], wgu.at[1, cc], w_sem.at[0, c]))
    for c in range(per):
        cc = pl.ds(lows[c], sizes[c])
        wcopies.append(pltpu.make_async_copy(wd_hbm.at[0, :, cc], wd.at[:, cc], w_sem.at[1, c]))
    for copy in wcopies:
        copy.start()

    tab[...] = jnp.zeros_like(tab)
    for copy in small:
        copy.wait()
    slot = lax.broadcasted_iota(jnp.int32, (n, rows), 0)
    flags = jnp.zeros((n, rows), jnp.int32)
    for e in range(n):
        flags = jnp.where(slot == e, flag_s[e], flags)
    for s in range(steps):
        served = slot if s == 0 else jnp.where(flags == 1, jnp.bitwise_xor(slot, 1), slot)
        ids, probs = ids_v[s], probs_v[s]
        shares = probs / jnp.sum(probs, axis=0, keepdims=True)
        table = jnp.zeros((n, rows), F32)
        for j in range(ids.shape[0]):
            table = jnp.where(ids[j : j + 1] == served, shares[j : j + 1], table)
        coarse = table.astype(BF16).astype(F32)
        tab[2 * s * n : (2 * s + 1) * n, 0:rows] = coarse
        tab[(2 * s + 1) * n : (2 * s + 2) * n, 0:rows] = table - coarse
    tok[0, k, y, z, :, width : width + LANES] = jnp.transpose(tab[...])[0:rows].astype(BF16)
    own.wait()
    pl.semaphore_wait(barrier, len(peers))

    def spot(u):
        s, c = u // per, u % per
        return s, c, pl.ds(lows[c], sizes[c])

    def carried(u):
        s, c = u // per, u % per
        last = s == 0 and c == per - 1
        return s, pl.ds(lows[c], sizes[c] + LANES if last else sizes[c]), c < GATHER_CROSSED[s]

    def extra_of(u):
        return sum(GATHER_CROSSED[: u // per]) + u % per

    def arrived(ref, sem):
        remote(ref, ref, sem, sem, sib).wait_recv()

    def block(u, kk, yy, zz):
        s, cc, _ = carried(u)
        return tok.at[s, kk, yy, zz, :, cc]

    def column(u, kk, yy):
        s, cc, _ = carried(u)
        return tok.at[s, kk, yy, :, :, cc]

    def along_z(u, yy, kind, recv, at):
        here = block(u, k, yy, z)
        for j in range(nz - 1):
            zz = source(j)
            copy = remote(here, here, sent.at[kind, u // per], recv.at[at, z], dev(zz, y, k))
            if RELAY:
                pl.when(jnp.logical_not((low & (zz == nz - 1)) | (high & (zz == 0))))(copy.start)
            else:
                copy.start()

    def issue_z(u):
        s, _, crossed = carried(u)
        along_z(u, y, 6 if crossed else 0, z_recv, u)
        if crossed:
            arrived(block(u, k, oy, z), y_recv.at[u])
            along_z(u, oy, 6, zx_recv, extra_of(u))

    def across_y(u, zz):
        here = block(u, k, y, zz)
        remote(here, here, sent.at[7 if carried(u)[2] else 1, u // per], y_recv.at[u], ynb).start()

    def issue_y(u):
        across_y(u, z)

    def arrive_z(u, yy, zs, kind, recv, at):
        here = block(u, k, yy, zs)
        arrived(here, recv.at[at, zs])
        if RELAY:
            passed = ((z == nz - 2) & (zs == 0)) | ((z == 1) & (zs == nz - 1))
            onward = dev(jnp.where(z == 1, 0, nz - 1), y, k)
            pl.when(passed)(remote(here, here, sent.at[kind, u // per], recv.at[at, zs], onward).start)

    def forward_from(u, j):
        crossed = carried(u)[2]
        zs = source(j)
        if crossed:
            arrive_z(u, y, zs, 6, z_recv, u)
            arrive_z(u, oy, zs, 6, zx_recv, extra_of(u))
        else:
            arrive_z(u, y, zs, 0, z_recv, u)
            across_y(u, zs)

    def forward(u):
        for j in range(nz - 2):
            forward_from(u, j)

    def forward_last(u):
        s, cc, crossed = carried(u)
        forward_from(u, nz - 2)
        if crossed:
            both = tok.at[s, k, :, :, :, cc]
            remote(both, both, sent.at[2, s], s_recv.at[u], sib).start()
        else:
            col = column(u, k, y)
            remote(col, col, sent.at[2, s], s_recv.at[u], sib).start()

    def forward_other(u):
        s, _, crossed = carried(u)
        if not crossed:
            col = column(u, k, oy)
            arrived(col, y_recv.at[u])
            remote(col, col, sent.at[2, s], s_recv.at[u], sib).start()

    def gate_up(u):
        s, c, cc = spot(u)
        _, wide, _ = carried(u)
        arrived(tok.at[s, ok, :, :, :, wide], s_recv.at[u])
        if s == 0:
            pltpu.make_async_copy(wgu.at[:, cc], wgu.at[:, cc], w_sem.at[0, c]).wait()
        lhs = tok[s, :, :, :, :, cc].reshape(n * rows, sizes[c])
        g = jnp.dot(lhs, wgu[0, cc, :], preferred_element_type=F32)
        up = jnp.dot(lhs, wgu[1, cc, :], preferred_element_type=F32)
        first = GATHER_CROSSED[s] % per
        if c != first:
            g = acc_g[...] + g
            up = acc_u[...] + up
        if c != (first - 1) % per:
            acc_g[...] = g
            acc_u[...] = up
        else:
            hid[...] = (g / (1.0 + jnp.exp(-g)) * up).astype(BF16)
            if s == 0:
                all_shares()

    def all_shares():
        table = tok[0, :, :, :, :, width : width + LANES].reshape(n * rows, LANES).astype(F32)
        lane = lax.broadcasted_iota(jnp.int32, (n * rows, LANES), 1)
        for s in range(steps):
            mine = (lane == 2 * s * n + me) | (lane == (2 * s + 1) * n + me)
            total = jnp.sum(jnp.where(mine, table, 0.0), axis=1, keepdims=True)
            share[s] = jnp.broadcast_to(total, (n * rows, LANES))

    def down(u):
        s, c, cc = spot(u)
        if s == 0:
            pltpu.make_async_copy(wd.at[:, cc], wd.at[:, cc], w_sem.at[1, c]).wait()
        res = jnp.dot(hid[...], wd[:, cc], preferred_element_type=F32)
        part[s, :, :, :, :, cc] = (res * share[s][:, 0:1]).astype(BF16).reshape(2, 2, nz, rows, sizes[c])
        remote(part.at[s, ok, :, :, :, cc], r1.at[s, :, :, :, cc], sent.at[3, s], r1_recv.at[u], sib).start()

    def add(*terms):
        total = terms[0].astype(F32)
        for term in terms[1:]:
            total = total + term.astype(F32)
        return total

    def back_z(u, yi, yy, kind, sem):
        s, _, cc = spot(u)
        for j in range(nz - 1):
            zz = nearest(j)
            place = jnp.where(z < zz, z, z - 1)
            remote(
                part.at[s, k, yy, zz, :, cc], r3.at[s, yi, place, :, cc],
                sent.at[kind, s], sem, dev(zz, y, k),
            ).start()

    def total_z(u, yi, yy, sem):
        s, _, cc = spot(u)
        arrived(r3.at[s, yi, :, :, cc], sem)
        return add(part[s, k, yy, z, :, cc], *(r3[s, yi, d, :, cc] for d in range(nz - 1)))

    def return_first(u):
        s, c, cc = spot(u)
        arrived(r1.at[s, :, :, :, cc], r1_recv.at[u])
        part[s, k, oy, :, :, cc] = add(part[s, k, oy, :, :, cc], r1[s, oy, :, :, cc]).astype(BF16)
        if c < RETURN_CROSSED[s]:
            back_z(u, 1, oy, 8, rx_recv.at[s, c])
            part[s, k, y, :, :, cc] = add(part[s, k, y, :, :, cc], r1[s, y, :, :, cc]).astype(BF16)
            back_z(u, 0, y, 8, r3_recv.at[u])
        else:
            remote(part.at[s, k, oy, :, :, cc], r2.at[s, :, :, cc], sent.at[4, s], r2_recv.at[u], ynb).start()

    def return_second(u):
        s, c, cc = spot(u)
        if c < RETURN_CROSSED[s]:
            part[s, k, oy, z, :, cc] = total_z(u, 1, oy, rx_recv.at[s, c]).astype(BF16)
            remote(part.at[s, k, oy, z, :, cc], r2.at[s, 0, :, cc], sent.at[9, s], r2_recv.at[u], ynb).start()
        else:
            arrived(r2.at[s, :, :, cc], r2_recv.at[u])
            part[s, k, y, :, :, cc] = add(
                part[s, k, y, :, :, cc], r1[s, y, :, :, cc], r2[s, :, :, cc]
            ).astype(BF16)
            back_z(u, 0, y, 5, r3_recv.at[u])

    def finish(u):
        s, c, cc = spot(u)
        total = total_z(u, 0, y, r3_recv.at[u])
        if c < RETURN_CROSSED[s]:
            arrived(r2.at[s, 0, :, cc], r2_recv.at[u])
            total = total + r2[s, 0, :, cc].astype(F32)
        outv[s, :, cc] = total.astype(BF16)
        pltpu.make_async_copy(outv.at[s, :, cc], out_hbm.at[s, :, cc], out_sem).start()

    stages = {
        "y": issue_y, "z": issue_z, "f": forward, "F": forward_last, "o": forward_other, "g": gate_up,
        "d": down, "2": return_first, "3": return_second, "5": finish,
    }
    for name, u in plan(steps, per):
        stages[name](u)

    def all_sent(kind, s, ref):
        remote(ref, ref, sent.at[kind, s], sent.at[kind, s], sib).wait_send()

    for s in range(steps):
        extra = LANES if s == 0 else 0
        split = lows[GATHER_CROSSED[s]]
        crossed, straight = pl.ds(0, split), pl.ds(split, width + extra - split)
        counts = [(None, nz - 1)]
        if RELAY:
            ends = low | high
            counts = [(ends, nz - 2), (relay, nz)]
            if nz > 4:
                counts.append((jnp.logical_not(ends | relay), nz - 1))
        for cond, count in counts:
            def sent_z(s=s, count=count, crossed=crossed, straight=straight, split=split):
                all_sent(0, s, tok.at[s, 0, 0, pl.ds(0, count), :, straight])
                if split:
                    all_sent(6, s, tok.at[s, 0, :, pl.ds(0, count), :, crossed])
            if cond is None:
                sent_z()
            else:
                pl.when(cond)(sent_z)
        all_sent(1, s, tok.at[s, 0, 0, :, :, straight])
        if split:
            all_sent(7, s, tok.at[s, 0, 0, 0, :, crossed])
        all_sent(2, s, tok.at[s, 0, :, :, :, pl.ds(0, width + extra)])
        all_sent(3, s, r1.at[s])
        split = lows[RETURN_CROSSED[s]]
        crossed, straight = pl.ds(0, split), pl.ds(split, width - split)
        all_sent(4, s, r2.at[s, :, :, straight])
        all_sent(5, s, r3.at[s, 0, :, :, straight])
        if split:
            all_sent(8, s, r3.at[s, :, :, :, crossed])
            all_sent(9, s, r2.at[s, 0, :, crossed])
    pltpu.make_async_copy(outv, outv, out_sem).wait()


def moe(n, x, ids, probs, flags, wg, wu, wd):
    steps, rows, width = x.shape
    hidden = wg.shape[2]
    nz = n // 4
    per = len(EIGHTHS)
    units = steps * per
    vm = pltpu.VMEM
    dma = pltpu.SemaphoreType.DMA
    anyspec = pl.BlockSpec(memory_space=pl.ANY)
    return pl.pallas_call(
        functools.partial(moe_kernel, n),
        out_shape=jax.ShapeDtypeStruct(x.shape, BF16),
        in_specs=[anyspec] * 7,
        out_specs=anyspec,
        scratch_shapes=[
            vm((steps, 2, 2, nz, rows, width + LANES), BF16),
            vm(ids.shape, jnp.int32),
            vm(probs.shape, F32),
            pltpu.SMEM(flags.shape, jnp.int32),
            vm((LANES, LANES), F32),
            vm((2, width, hidden), BF16),
            vm((hidden, width), BF16),
            vm((n * rows, hidden), F32),
            vm((n * rows, hidden), F32),
            vm((n * rows, hidden), BF16),
            vm((steps, n * rows, LANES), F32),
            vm((steps, 2, 2, nz, rows, width), BF16),
            vm((steps, 2, nz, rows, width), BF16),
            vm((steps, nz, rows, width), BF16),
            vm((steps, 2, nz - 1, rows, width), BF16),
            vm((steps, rows, width), BF16),
            dma((10, steps)), dma((units, nz)), dma((sum(GATHER_CROSSED), nz)), dma((units,)), dma((units,)),
            dma((units,)), dma((units,)), dma((units,)), dma((steps, max(RETURN_CROSSED))), dma((2, per)), dma((4,)), dma,
        ],
        compiler_params=pltpu.CompilerParams(
            collective_id=0, has_side_effects=True, vmem_limit_bytes=67000000
        ),
    )(x, ids, probs, flags, wg, wu, wd)


def on_device(hidden_states, expert_ids, router_probs, swap_flags, w_gate, w_up, w_down):
    n = lax.axis_size("expert")
    ids = jnp.swapaxes(expert_ids, 1, 2)
    probs = jnp.swapaxes(router_probs, 1, 2)
    return moe(n, hidden_states, ids, probs, swap_flags, w_gate, w_up, w_down)


def solution(mesh):
    return jax.shard_map(
        on_device,
        mesh=mesh,
        in_specs=(
            P(None, ("groups", "expert"), None),
            P(None, ("groups", "expert"), None),
            P(None, ("groups", "expert"), None),
            P(),
            P("expert", None, None),
            P("expert", None, None),
            P("expert", None, None),
        ),
        out_specs=P(None, ("groups", "expert"), None),
        check_vma=False,
    )
```

```python
import functools

import jax
import jax.numpy as jnp
from jax import lax
from jax.experimental import pallas as pl
from jax.experimental.pallas import tpu as pltpu
from jax.sharding import PartitionSpec as P

MESH = pl.DeviceIdType.MESH
F32 = jnp.float32
BF16 = jnp.bfloat16
LANES = 128
RELAY = True
EIGHTHS = (2, 2, 2, 2)
GATHER_CROSSED = (1, 1)
RETURN_CROSSED = (1, 0)
LAG, OLAG = 3, 2
AHEAD, YOWN = 3, 1


def plan(steps, per):
    units = steps * per
    gather, back = [], []
    for s in range(steps):
        first, rest = range(GATHER_CROSSED[s]), range(GATHER_CROSSED[s], per)
        gather.append([s * per + c for c in (*rest, *first)])
        first, rest = range(RETURN_CROSSED[s]), range(RETURN_CROSSED[s], per)
        back.append([s * per + c for c in (*first, *rest)])
    old, new = back
    seq = []
    order = gather[0] + gather[1]
    own = [gather[s][per - GATHER_CROSSED[s] :] + gather[s][: per - GATHER_CROSSED[s]] for s in range(steps)]
    lag = LAG
    seq += [("y", u) for u in own[0]]
    seq += [("z", u) for u in order[:AHEAD]]
    for t in range(units):
        if t == YOWN:
            seq += [("y", u) for u in own[1]]
        seq.append(("f", order[t]))
        if t + AHEAD < units and (t > 0 or AHEAD < per):
            seq.append(("z", order[t + AHEAD]))
        if t == per + lag - 1:
            seq.append(("g", order[per - 1]))
            seq += [("d", u) for u in old[:2]]
        if 1 <= t:
            seq.append(("F", order[t - 1]))
        if t == units - 1:
            seq += [("2", old[0]), ("2", old[1])]
        if OLAG <= t:
            seq.append(("o", order[t - OLAG]))
        if lag <= t < per + lag - 1:
            seq.append(("g", order[t - lag]))
    seq += [("d", u) for u in old[2:]]
    seq += [("F", order[units - 1])]
    seq += [("2", u) for u in old[2:]]
    seq += [("o", order[t]) for t in range(units - OLAG, units)]
    a, b, c, d = old
    e, f, g, h = new
    if RETURN_CROSSED[0]:
        a, b, c, d = b, c, a, d
    last = gather[1]
    seq += [("g", last[0]), ("g", last[1]), ("g", last[2]), ("3", a), ("g", last[3]), ("d", e), ("d", f), ("3", b)]
    seq += [("2", e), ("d", g), ("2", f), ("d", h), ("2", g), ("3", d), ("2", h), ("3", c)]
    seq += [("3", e), ("5", a), ("5", b), ("3", f), ("5", d), ("3", g), ("5", e), ("3", h), ("5", c)]
    seq += [("5", f), ("5", g), ("5", h)]
    return seq


def moe_kernel(
    n, x_hbm, ids_hbm, probs_hbm, flag_hbm, wg_hbm, wu_hbm, wd_hbm, out_hbm,
    tok, ids_v, probs_v, flag_s, tab, wgu, wd, acc_g, acc_u, hid, share, part, r1, r2, r3, outv,
    sent, z_recv, zx_recv, y_recv, s_recv, r1_recv, r2_recv, r3_recv, rx_recv, w_sem, in_sem, out_sem,
):
    nz = n // 4
    steps, rows, width = x_hbm.shape
    per = len(EIGHTHS)
    sizes = [part_of * width // 8 for part_of in EIGHTHS]
    lows = [sum(sizes[:c]) for c in range(per + 1)]
    units = steps * per
    me = lax.axis_index("expert")
    k = lax.rem(me, 2)
    y = lax.rem(lax.div(me, 2), 2)
    z = lax.div(me, 4)
    ok, oy = 1 - k, 1 - y
    low, high = z == 0, z == nz - 1
    relay = (z == 1) | (z == nz - 2)

    def zat(d):
        return lax.rem(z + d + nz, nz)

    def nearest(j):
        up = jnp.where(j < z, j, j + 1)
        down = jnp.where(nz - 1 - j > z, nz - 1 - j, nz - 2 - j)
        return jnp.where(z < nz // 2, up, down)

    def source(j):
        return jnp.where(relay, nearest((j + nz - 2) % (nz - 1)), nearest(j)) if RELAY else nearest(j)

    def dev(zz, yy, kk):
        return {"expert": zz * 4 + yy * 2 + kk}

    def remote(src, dst, ss, rs, target):
        return pltpu.make_async_remote_copy(
            src_ref=src, dst_ref=dst, send_sem=ss, recv_sem=rs,
            device_id=target, device_id_type=MESH,
        )

    sib = dev(z, y, ok)
    ynb = dev(z, oy, k)

    barrier = pltpu.get_barrier_semaphore()
    peers = [sib, ynb] + [dev(zat(d), y, k) for d in range(1, nz)]
    for peer in peers:
        pl.semaphore_signal(barrier, inc=1, device_id=peer, device_id_type=MESH)

    small = [
        pltpu.make_async_copy(ids_hbm, ids_v, in_sem.at[0]),
        pltpu.make_async_copy(probs_hbm, probs_v, in_sem.at[1]),
        pltpu.make_async_copy(flag_hbm, flag_s, in_sem.at[2]),
    ]
    own = pltpu.make_async_copy(x_hbm, tok.at[:, k, y, z, :, pl.ds(0, width)], in_sem.at[3])
    for copy in small + [own]:
        copy.start()
    wcopies = []
    for c in range(per):
        cc = pl.ds(lows[c], sizes[c])
        wcopies.append(pltpu.make_async_copy(wg_hbm.at[0, cc], wgu.at[0, cc], w_sem.at[0, c]))
        wcopies.append(pltpu.make_async_copy(wu_hbm.at[0, cc], wgu.at[1, cc], w_sem.at[0, c]))
    for c in range(per):
        cc = pl.ds(lows[c], sizes[c])
        wcopies.append(pltpu.make_async_copy(wd_hbm.at[0, :, cc], wd.at[:, cc], w_sem.at[1, c]))
    for copy in wcopies:
        copy.start()

    tab[...] = jnp.zeros_like(tab)
    for copy in small:
        copy.wait()
    slot = lax.broadcasted_iota(jnp.int32, (n, rows), 0)
    flags = jnp.zeros((n, rows), jnp.int32)
    for e in range(n):
        flags = jnp.where(slot == e, flag_s[e], flags)
    for s in range(steps):
        served = slot if s == 0 else jnp.where(flags == 1, jnp.bitwise_xor(slot, 1), slot)
        ids, probs = ids_v[s], probs_v[s]
        shares = probs / jnp.sum(probs, axis=0, keepdims=True)
        table = jnp.zeros((n, rows), F32)
        for j in range(ids.shape[0]):
            table = jnp.where(ids[j : j + 1] == served, shares[j : j + 1], table)
        coarse = table.astype(BF16).astype(F32)
        tab[2 * s * n : (2 * s + 1) * n, 0:rows] = coarse
        tab[(2 * s + 1) * n : (2 * s + 2) * n, 0:rows] = table - coarse
    tok[0, k, y, z, :, width : width + LANES] = jnp.transpose(tab[...])[0:rows].astype(BF16)
    own.wait()
    pl.semaphore_wait(barrier, len(peers))

    def spot(u):
        s, c = u // per, u % per
        return s, c, pl.ds(lows[c], sizes[c])

    def carried(u):
        s, c = u // per, u % per
        last = s == 0 and c == per - 1
        return s, pl.ds(lows[c], sizes[c] + LANES if last else sizes[c]), c < GATHER_CROSSED[s]

    def extra_of(u):
        return sum(GATHER_CROSSED[: u // per]) + u % per

    def arrived(ref, sem):
        remote(ref, ref, sem, sem, sib).wait_recv()

    def block(u, kk, yy, zz):
        s, cc, _ = carried(u)
        return tok.at[s, kk, yy, zz, :, cc]

    def column(u, kk, yy):
        s, cc, _ = carried(u)
        return tok.at[s, kk, yy, :, :, cc]

    def along_z(u, yy, kind, recv, at):
        here = block(u, k, yy, z)
        for j in range(nz - 1):
            zz = source(j)
            copy = remote(here, here, sent.at[kind, u // per], recv.at[at, z], dev(zz, y, k))
            if RELAY:
                pl.when(jnp.logical_not((low & (zz == nz - 1)) | (high & (zz == 0))))(copy.start)
            else:
                copy.start()

    def issue_z(u):
        s, _, crossed = carried(u)
        along_z(u, y, 6 if crossed else 0, z_recv, u)
        if crossed:
            arrived(block(u, k, oy, z), y_recv.at[u])
            along_z(u, oy, 6, zx_recv, extra_of(u))

    def across_y(u, zz):
        here = block(u, k, y, zz)
        remote(here, here, sent.at[7 if carried(u)[2] else 1, u // per], y_recv.at[u], ynb).start()

    def issue_y(u):
        across_y(u, z)

    def arrive_z(u, yy, zs, kind, recv, at):
        here = block(u, k, yy, zs)
        arrived(here, recv.at[at, zs])
        if RELAY:
            passed = ((z == nz - 2) & (zs == 0)) | ((z == 1) & (zs == nz - 1))
            onward = dev(jnp.where(z == 1, 0, nz - 1), y, k)
            pl.when(passed)(remote(here, here, sent.at[kind, u // per], recv.at[at, zs], onward).start)

    def forward_from(u, j):
        crossed = carried(u)[2]
        zs = source(j)
        if crossed:
            arrive_z(u, y, zs, 6, z_recv, u)
            arrive_z(u, oy, zs, 6, zx_recv, extra_of(u))
        else:
            arrive_z(u, y, zs, 0, z_recv, u)
            across_y(u, zs)

    def forward(u):
        for j in range(nz - 2):
            forward_from(u, j)

    def forward_last(u):
        s, cc, crossed = carried(u)
        forward_from(u, nz - 2)
        if crossed:
            both = tok.at[s, k, :, :, :, cc]
            remote(both, both, sent.at[2, s], s_recv.at[u], sib).start()
        else:
            col = column(u, k, y)
            remote(col, col, sent.at[2, s], s_recv.at[u], sib).start()

    def forward_other(u):
        s, _, crossed = carried(u)
        if not crossed:
            col = column(u, k, oy)
            arrived(col, y_recv.at[u])
            remote(col, col, sent.at[2, s], s_recv.at[u], sib).start()

    def gate_up(u):
        s, c, cc = spot(u)
        _, wide, _ = carried(u)
        arrived(tok.at[s, ok, :, :, :, wide], s_recv.at[u])
        if s == 0:
            pltpu.make_async_copy(wgu.at[:, cc], wgu.at[:, cc], w_sem.at[0, c]).wait()
        lhs = tok[s, :, :, :, :, cc].reshape(n * rows, sizes[c])
        g = jnp.dot(lhs, wgu[0, cc, :], preferred_element_type=F32)
        up = jnp.dot(lhs, wgu[1, cc, :], preferred_element_type=F32)
        first = GATHER_CROSSED[s] % per
        if c != first:
            g = acc_g[...] + g
            up = acc_u[...] + up
        if c != (first - 1) % per:
            acc_g[...] = g
            acc_u[...] = up
        else:
            hid[...] = (g / (1.0 + jnp.exp(-g)) * up).astype(BF16)
            if s == 0:
                all_shares()

    def all_shares():
        table = tok[0, :, :, :, :, width : width + LANES].reshape(n * rows, LANES).astype(F32)
        lane = lax.broadcasted_iota(jnp.int32, (n * rows, LANES), 1)
        for s in range(steps):
            mine = (lane == 2 * s * n + me) | (lane == (2 * s + 1) * n + me)
            total = jnp.sum(jnp.where(mine, table, 0.0), axis=1, keepdims=True)
            share[s] = jnp.broadcast_to(total, (n * rows, LANES))

    def down(u):
        s, c, cc = spot(u)
        if s == 0:
            pltpu.make_async_copy(wd.at[:, cc], wd.at[:, cc], w_sem.at[1, c]).wait()
        res = jnp.dot(hid[...], wd[:, cc], preferred_element_type=F32)
        part[s, :, :, :, :, cc] = (res * share[s][:, 0:1]).astype(BF16).reshape(2, 2, nz, rows, sizes[c])
        remote(part.at[s, ok, :, :, :, cc], r1.at[s, :, :, :, cc], sent.at[3, s], r1_recv.at[u], sib).start()

    def add(*terms):
        total = terms[0].astype(F32)
        for term in terms[1:]:
            total = total + term.astype(F32)
        return total

    def back_z(u, yi, yy, kind, sem):
        s, _, cc = spot(u)
        for j in range(nz - 1):
            zz = nearest(j)
            place = jnp.where(z < zz, z, z - 1)
            remote(
                part.at[s, k, yy, zz, :, cc], r3.at[s, yi, place, :, cc],
                sent.at[kind, s], sem, dev(zz, y, k),
            ).start()

    def total_z(u, yi, yy, sem):
        s, _, cc = spot(u)
        arrived(r3.at[s, yi, :, :, cc], sem)
        return add(part[s, k, yy, z, :, cc], *(r3[s, yi, d, :, cc] for d in range(nz - 1)))

    def return_first(u):
        s, c, cc = spot(u)
        arrived(r1.at[s, :, :, :, cc], r1_recv.at[u])
        part[s, k, oy, :, :, cc] = add(part[s, k, oy, :, :, cc], r1[s, oy, :, :, cc]).astype(BF16)
        if c < RETURN_CROSSED[s]:
            back_z(u, 1, oy, 8, rx_recv.at[s, c])
            part[s, k, y, :, :, cc] = add(part[s, k, y, :, :, cc], r1[s, y, :, :, cc]).astype(BF16)
            back_z(u, 0, y, 8, r3_recv.at[u])
        else:
            remote(part.at[s, k, oy, :, :, cc], r2.at[s, :, :, cc], sent.at[4, s], r2_recv.at[u], ynb).start()

    def return_second(u):
        s, c, cc = spot(u)
        if c < RETURN_CROSSED[s]:
            part[s, k, oy, z, :, cc] = total_z(u, 1, oy, rx_recv.at[s, c]).astype(BF16)
            remote(part.at[s, k, oy, z, :, cc], r2.at[s, 0, :, cc], sent.at[9, s], r2_recv.at[u], ynb).start()
        else:
            arrived(r2.at[s, :, :, cc], r2_recv.at[u])
            part[s, k, y, :, :, cc] = add(
                part[s, k, y, :, :, cc], r1[s, y, :, :, cc], r2[s, :, :, cc]
            ).astype(BF16)
            back_z(u, 0, y, 5, r3_recv.at[u])

    def finish(u):
        s, c, cc = spot(u)
        total = total_z(u, 0, y, r3_recv.at[u])
        if c < RETURN_CROSSED[s]:
            arrived(r2.at[s, 0, :, cc], r2_recv.at[u])
            total = total + r2[s, 0, :, cc].astype(F32)
        outv[s, :, cc] = total.astype(BF16)
        pltpu.make_async_copy(outv.at[s, :, cc], out_hbm.at[s, :, cc], out_sem).start()

    stages = {
        "y": issue_y, "z": issue_z, "f": forward, "F": forward_last, "o": forward_other, "g": gate_up,
        "d": down, "2": return_first, "3": return_second, "5": finish,
    }
    stage_list = plan(steps, per)
    for name, u in stage_list[:-1]:
        stages[name](u)

    def all_sent(kind, s, ref):
        remote(ref, ref, sent.at[kind, s], sent.at[kind, s], sib).wait_send()

    for s in range(steps):
        extra = LANES if s == 0 else 0
        split = lows[GATHER_CROSSED[s]]
        crossed, straight = pl.ds(0, split), pl.ds(split, width + extra - split)
        counts = [(None, nz - 1)]
        if RELAY:
            ends = low | high
            counts = [(ends, nz - 2), (relay, nz)]
            if nz > 4:
                counts.append((jnp.logical_not(ends | relay), nz - 1))
        for cond, count in counts:
            def sent_z(s=s, count=count, crossed=crossed, straight=straight, split=split):
                all_sent(0, s, tok.at[s, 0, 0, pl.ds(0, count), :, straight])
                if split:
                    all_sent(6, s, tok.at[s, 0, :, pl.ds(0, count), :, crossed])
            if cond is None:
                sent_z()
            else:
                pl.when(cond)(sent_z)
        all_sent(1, s, tok.at[s, 0, 0, :, :, straight])
        if split:
            all_sent(7, s, tok.at[s, 0, 0, 0, :, crossed])
        all_sent(2, s, tok.at[s, 0, :, :, :, pl.ds(0, width + extra)])
        all_sent(3, s, r1.at[s])
        split = lows[RETURN_CROSSED[s]]
        crossed, straight = pl.ds(0, split), pl.ds(split, width - split)
        all_sent(4, s, r2.at[s, :, :, straight])
        all_sent(5, s, r3.at[s, 0, :, :, straight])
        if split:
            all_sent(8, s, r3.at[s, :, :, :, crossed])
            all_sent(9, s, r2.at[s, 0, :, crossed])
    name, u = stage_list[-1]
    stages[name](u)
    pltpu.make_async_copy(outv, outv, out_sem).wait()


def moe(n, x, ids, probs, flags, wg, wu, wd):
    steps, rows, width = x.shape
    hidden = wg.shape[2]
    nz = n // 4
    per = len(EIGHTHS)
    units = steps * per
    vm = pltpu.VMEM
    dma = pltpu.SemaphoreType.DMA
    anyspec = pl.BlockSpec(memory_space=pl.ANY)
    return pl.pallas_call(
        functools.partial(moe_kernel, n),
        out_shape=jax.ShapeDtypeStruct(x.shape, BF16),
        in_specs=[anyspec] * 7,
        out_specs=anyspec,
        scratch_shapes=[
            vm((steps, 2, 2, nz, rows, width + LANES), BF16),
            vm(ids.shape, jnp.int32),
            vm(probs.shape, F32),
            pltpu.SMEM(flags.shape, jnp.int32),
            vm((LANES, LANES), F32),
            vm((2, width, hidden), BF16),
            vm((hidden, width), BF16),
            vm((n * rows, hidden), F32),
            vm((n * rows, hidden), F32),
            vm((n * rows, hidden), BF16),
            vm((steps, n * rows, LANES), F32),
            vm((steps, 2, 2, nz, rows, width), BF16),
            vm((steps, 2, nz, rows, width), BF16),
            vm((steps, nz, rows, width), BF16),
            vm((steps, 2, nz - 1, rows, width), BF16),
            vm((steps, rows, width), BF16),
            dma((10, steps)), dma((units, nz)), dma((sum(GATHER_CROSSED), nz)), dma((units,)), dma((units,)),
            dma((units,)), dma((units,)), dma((units,)), dma((steps, max(RETURN_CROSSED))), dma((2, per)), dma((4,)), dma,
        ],
        compiler_params=pltpu.CompilerParams(
            collective_id=0, has_side_effects=True, vmem_limit_bytes=67000000
        ),
    )(x, ids, probs, flags, wg, wu, wd)


def on_device(hidden_states, expert_ids, router_probs, swap_flags, w_gate, w_up, w_down):
    n = lax.axis_size("expert")
    ids = jnp.swapaxes(expert_ids, 1, 2)
    probs = jnp.swapaxes(router_probs, 1, 2)
    return moe(n, hidden_states, ids, probs, swap_flags, w_gate, w_up, w_down)


def solution(mesh):
    return jax.shard_map(
        on_device,
        mesh=mesh,
        in_specs=(
            P(None, ("groups", "expert"), None),
            P(None, ("groups", "expert"), None),
            P(None, ("groups", "expert"), None),
            P(),
            P("expert", None, None),
            P("expert", None, None),
            P("expert", None, None),
        ),
        out_specs=P(None, ("groups", "expert"), None),
        check_vma=False,
    )
```
